32 devices in a mesh: dp: 16 (over z, y, core), fsdp: 2 (over x).
Axes of the slice: x: 2, y: 2, z: 4, core: 2. Of those that a mesh axis runs over, the one named last changes fastest.
Arguments:
- frames: bfloat16 [2, 16384, 512], P(None, ('dp', 'fsdp')), may hold values from -6 to 6
- item_lengths: int32 [2, 32, 8], P(None, ('dp', 'fsdp')), may hold values from 1 to 384, 512 in all within a row
- frame_mask: int32 [2, 16384], P(None, ('dp', 'fsdp')), may hold values 0 or 1
- first_norm: bfloat16 [512], P('fsdp'), may hold values from 0.5 to 1.5
- first_up: bfloat16 [512, 2048], P('fsdp'), may hold values from -0.25 to 0.25
- first_down: bfloat16 [2048, 512], P('fsdp'), may hold values from -0.125 to 0.125
- attend_norm: bfloat16 [512], P('fsdp'), may hold values from 0.5 to 1.5
- attend_joint: bfloat16 [512, 1536], P('fsdp'), may hold values from -0.25 to 0.25
- attend_out: bfloat16 [512, 512], P('fsdp'), may hold values from -1 to 1
- conv_norm: bfloat16 [512], P('fsdp'), may hold values from 0.5 to 1.5
- conv_in: bfloat16 [512, 1024], P('fsdp'), may hold values from -0.25 to 0.25
- conv_kernel: bfloat16 [32, 512], P('fsdp'), may hold values from -1 to 1
- batch_gain: bfloat16 [512], P('fsdp'), may hold values from 0.5 to 1.5
- batch_bias: bfloat16 [512], P('fsdp'), may hold values from -3 to 3
- conv_out: bfloat16 [512, 512], P('fsdp'), may hold values from -0.25 to 0.25
- second_norm: bfloat16 [512], P('fsdp'), may hold values from 0.5 to 1.5
- second_up: bfloat16 [512, 2048], P('fsdp'), may hold values from -0.25 to 0.25
- second_down: bfloat16 [2048, 512], P('fsdp'), may hold values from -0.125 to 0.125
- final_norm: bfloat16 [512], P('fsdp'), may hold values from 0.5 to 1.5
- output_grad: bfloat16 [2, 16384, 512], P(None, ('dp', 'fsdp')), may hold values from -6 to 6
Outputs:
- encoded: bfloat16 [2, 16384, 512], P(None, ('dp', 'fsdp'))
- frames_grad: bfloat16 [2, 16384, 512], P(None, ('dp', 'fsdp'))
- first_norm_grad: float32 [512], P('fsdp')
- first_up_grad: float32 [512, 2048], P('fsdp')
- first_down_grad: float32 [2048, 512], P('fsdp')
- attend_norm_grad: float32 [512], P('fsdp')
- attend_joint_grad: float32 [512, 1536], P('fsdp')
- attend_out_grad: float32 [512, 512], P('fsdp')
- conv_norm_grad: float32 [512], P('fsdp')
- conv_in_grad: float32 [512, 1024], P('fsdp')
- conv_kernel_grad: float32 [32, 512], P('fsdp')
- batch_gain_grad: float32 [512], P('fsdp')
- batch_bias_grad: float32 [512], P('fsdp')
- conv_out_grad: float32 [512, 512], P('fsdp')
- second_norm_grad: float32 [512], P('fsdp')
- second_up_grad: float32 [512, 2048], P('fsdp')
- second_down_grad: float32 [2048, 512], P('fsdp')
- final_norm_grad: float32 [512], P('fsdp')
The draws below stay inside these ranges and needn't reach their ends.
Inputs may be any that keep to these rules, and one draw needn't show every extreme that they name: `item_lengths`: each row of 8 lengths sums to 512; its largest is exactly 384.
All inputs are finite; a program needn't handle non-finite values. No bound on the sum of `frame_mask` on one device may be relied on, other than what follows from the above.
Results may differ from the reference program's by a relative error of at most 0.019.
Values may be sent and summed in bfloat16 or wider, within the bound.
No kernel may reach another device: no remote copies, remote signals or barrier semaphores. Data moves between devices by JAX's collectives and lax.ppermute only.
A program may use at most 192 MiB of HBM per device.

```python
import math
import jax
import jax.numpy as jnp
import numpy as np
from jax import lax

D = 512
FF = 2048
HEADS = 8
KER = 32
HDIM = 64
SLOTS = 512
ITEMS = 8
MB = 2
LONGEST = 384
TOK = 16384
DEVICES = 32


def plant(values, rng, least, largest):
    spot = [jax.random.randint(jax.random.fold_in(rng, axis), (), 0, length) for axis, length in enumerate(values.shape)]
    widest = values.shape.index(max(values.shape))
    next_to = spot[:widest] + [(spot[widest] + 1) % values.shape[widest]] + spot[widest + 1:]
    return values.at[tuple(spot)].set(least).at[tuple(next_to)].set(largest)


def levels(stream_key, extent, cuts, low, high):
    factor_of, own = 1.0, jax.random.fold_in(stream_key, 6)
    for axis_at, parts in cuts:
        draws = jnp.exp(jax.random.uniform(jax.random.fold_in(own, axis_at), (parts,), jnp.float32, low / len(cuts), high / len(cuts)))
        factor_of = factor_of * jnp.repeat(draws, extent[axis_at] // parts).reshape([-1 if axis == axis_at else 1 for axis in range(len(extent))])
    return factor_of


def length_profile(count, total, most, lean):
    weights = [(1 << 20) // math.isqrt(grade ** lean) + 1 for grade in range(2, count + 1)]
    rest, given = total - most - (count - 1), [1] * (count - 1)
    while rest > 0:
        free = [i for i in range(count - 1) if given[i] < most]
        whole, budget = sum([weights[i] for i in free]), rest
        for i in free:
            addition = min(most - given[i], max(1, budget * weights[i] // whole), rest)
            given[i] = given[i] + addition
            rest = rest - addition
    return np.array([most] + given)


def ragged_sizes(rng, amount, total, reach, lean):
    if amount == 2:
        one = jax.random.randint(rng, (), max(1, total - reach), min(reach, total - 1) + 1)
        return jnp.stack([one, total - one])
    sizes = jnp.asarray(length_profile(amount, total, reach, lean), jnp.int32)
    couples = (amount - 1) // 2
    giver, taker = sizes[1:1 + 2 * couples:2], sizes[2:2 + 2 * couples:2]
    margin = jnp.minimum(giver - 1, reach - taker)
    moved = jax.random.randint(jax.random.fold_in(rng, 1), (couples,), 0, 1 << 20) % (margin + 1)
    sizes = sizes.at[1:1 + 2 * couples:2].set(giver - moved).at[2:2 + 2 * couples:2].set(taker + moved)
    return sizes[jax.random.permutation(jax.random.fold_in(rng, 2), amount)]


def centred(rng, shape, width, bound, shards=(), kind=jnp.bfloat16):
    array = jax.random.normal(rng, shape, jnp.float32) * width
    if len(shards) > 0:
        array = levels(rng, shape, shards, -0.22, 0.18) * array
    return jnp.clip(array, min=-bound, max=bound).astype(kind)


def setup_inputs(seed: int = 0) -> dict:
    splits = jax.random.split(jax.random.key(seed), 21)
    frames = centred(splits[0], (MB, TOK, D), 1.0, 6.0, ((1, 32),))
    item_lengths = jax.vmap(lambda own: ragged_sizes(own, ITEMS, SLOTS, LONGEST, 2))(jax.random.split(splits[1], MB * DEVICES)).reshape((MB, DEVICES, ITEMS)).astype(jnp.int32)
    frame_mask = plant((jax.random.randint(splits[2], (MB, TOK), 0, 8) < 7).astype(jnp.int32), jax.random.fold_in(splits[2], 1), 0, 1)
    first_norm = jnp.clip(1.0 + 0.1 * jax.random.normal(splits[3], (D,), jnp.float32), 0.5, 1.5).astype(jnp.bfloat16)
    first_up = centred(splits[4], (D, FF), D ** -0.5, 0.25, ((0, 2),))
    first_down = centred(splits[5], (FF, D), FF ** -0.5, 0.125, ((0, 2),))
    attend_norm = jnp.clip(1.0 + 0.1 * jax.random.normal(splits[6], (D,), jnp.float32), 0.5, 1.5).astype(jnp.bfloat16)
    attend_joint = centred(splits[7], (D, 3 * D), D ** -0.5, 0.25, ((0, 2),))
    attend_out = centred(splits[8], (D, D), (D // 16) ** -0.5, 1.0, ((0, 2),))
    conv_norm = jnp.clip(1.0 + 0.1 * jax.random.normal(splits[9], (D,), jnp.float32), 0.5, 1.5).astype(jnp.bfloat16)
    conv_in = centred(splits[10], (D, 2 * D), D ** -0.5, 0.25, ((0, 2),))
    conv_kernel = centred(splits[11], (KER, D), KER ** -0.5, 1.0, ((0, 2),))
    batch_gain = jnp.clip(1.0 + 0.1 * jax.random.normal(splits[12], (D,), jnp.float32), 0.5, 1.5).astype(jnp.bfloat16)
    batch_bias = centred(splits[13], (D,), 0.5, 3.0, ((0, 2),))
    conv_out = centred(splits[14], (D, D), D ** -0.5, 0.25, ((0, 2),))
    second_norm = jnp.clip(1.0 + 0.1 * jax.random.normal(splits[15], (D,), jnp.float32), 0.5, 1.5).astype(jnp.bfloat16)
    second_up = centred(splits[16], (D, FF), D ** -0.5, 0.25, ((0, 2),))
    second_down = centred(splits[17], (FF, D), FF ** -0.5, 0.125, ((0, 2),))
    final_norm = jnp.clip(1.0 + 0.1 * jax.random.normal(splits[18], (D,), jnp.float32), 0.5, 1.5).astype(jnp.bfloat16)
    output_grad = centred(splits[19], (MB, TOK, D), 1.0, 6.0, ((1, 32),))
    return {"frames": frames, "item_lengths": item_lengths, "frame_mask": frame_mask, "first_norm": first_norm, "first_up": first_up, "first_down": first_down, "attend_norm": attend_norm, "attend_joint": attend_joint, "attend_out": attend_out, "conv_norm": conv_norm, "conv_in": conv_in, "conv_kernel": conv_kernel, "batch_gain": batch_gain, "batch_bias": batch_bias, "conv_out": conv_out, "second_norm": second_norm, "second_up": second_up, "second_down": second_down, "final_norm": final_norm, "output_grad": output_grad}


EPS = 1e-05
HIGH = lax.Precision.HIGHEST

@jax.custom_vjp
def low(v):
    return lax.optimization_barrier(v.astype(jnp.bfloat16)).astype(jnp.float32)

@jax.custom_vjp
def low_back(v):
    return v

def low_keep(v):
    return (low(v), None)

def low_pass(kept, grad):
    return (grad,)

def back_keep(v):
    return (v, None)

def back_low(kept, grad):
    return (low(grad),)
low.defvjp(low_keep, low_pass)
low_back.defvjp(back_keep, back_low)

def matmul(left, right):
    return jnp.dot(left, right, preferred_element_type=jnp.float32, precision=HIGH)

def layer_norm(values, gain):
    centered = values - lax.optimization_barrier(jnp.mean(values, axis=-1, keepdims=True))
    spread = lax.optimization_barrier(jnp.mean(centered * centered, axis=-1, keepdims=True))
    return centered * lax.rsqrt(spread + EPS) * gain

def swish(values):
    return values * jax.nn.sigmoid(values)

def frame_layout(lengths):
    lengths = lengths.astype(jnp.int32)
    ends = jnp.cumsum(lengths).astype(jnp.int32)
    starts = (ends - lengths).astype(jnp.int32)
    slot_ids = jnp.arange(SLOTS, dtype=jnp.int32)
    segment = lax.optimization_barrier(jnp.sum((slot_ids[:, None] >= ends[None, :]).astype(jnp.int32), axis=1)).astype(jnp.int32)
    member = segment[:, None] == jnp.arange(ITEMS, dtype=jnp.int32)[None, :]
    begin = lax.optimization_barrier(jnp.sum(jnp.where(member, starts[None, :], 0), axis=1)).astype(jnp.int32)
    return (segment, (slot_ids - begin).astype(jnp.int32))

def rotate(values, position, sign):
    half = HDIM // 2
    freq = jnp.exp(jnp.arange(half, dtype=jnp.float32) * (-2.0 * math.log(10000.0) / HDIM))
    angle = position.astype(jnp.float32)[:, None] * freq[None, :]
    cosine = jnp.cos(angle)[:, None, :]
    sine = sign * jnp.sin(angle)[:, None, :]
    first = values[..., :half]
    second = values[..., half:]
    return jnp.concatenate([first * cosine - second * sine, first * sine + second * cosine], axis=-1)

def feed(values, gain, w_up, w_down):
    entry_value = low(layer_norm(values, gain))
    inner = low_back(matmul(entry_value, w_up))
    hidden = low(swish(inner))
    return low_back(matmul(hidden, w_down))

def attend_device(pieces):
    query, keys, values, segment, valid_frames = pieces
    scores = low_back(jnp.einsum('qhd,khd->hqk', query, keys, precision=HIGH))
    slot_ids = jnp.arange(SLOTS, dtype=jnp.int32)
    allowed = (segment[:, None] == segment[None, :]) & ((valid_frames[None, :] > 0) | (slot_ids[:, None] == slot_ids[None, :]))
    masked = jnp.where(allowed[None, :, :], scores, -1000000000.0)
    shifted = masked - lax.optimization_barrier(jnp.max(masked, axis=-1, keepdims=True))
    expo = jnp.exp(shifted)
    probs = low(expo / lax.optimization_barrier(jnp.sum(expo, axis=-1, keepdims=True)))
    return low_back(jnp.einsum('hqk,khd->qhd', probs, values, precision=HIGH))

def attention(values, gain, w_joint, w_out, segment, position, valid_frames):
    entry_value = low(layer_norm(values, gain))
    joint_projection = low_back(matmul(entry_value, w_joint)).reshape(DEVICES, SLOTS, 3, HEADS, HDIM)
    turn = jax.vmap(rotate, in_axes=(0, 0, None))
    query = low(turn(joint_projection[:, :, 0], position, 1.0) * HDIM ** (-0.5))
    keys = low(turn(joint_projection[:, :, 1], position, 1.0))
    vals = low(joint_projection[:, :, 2])
    mixed_rows = lax.map(jax.checkpoint(attend_device), (query, keys, vals, segment, valid_frames.reshape(DEVICES, SLOTS)))
    output = low(mixed_rows.reshape(DEVICES * SLOTS, D))
    return low_back(matmul(output, w_out))

def depthwise(gated_linear_unit, segment, kernel):
    half = (KER - 1) // 2
    padded = jnp.pad(gated_linear_unit, ((0, 0), (KER, KER), (0, 0)))
    seg_pad = jnp.pad(segment, ((0, 0), (KER, KER)), constant_values=-1)
    total = jnp.zeros_like(gated_linear_unit)
    for offset in range(KER):
        begin = KER + offset - half
        piece = padded[:, begin:begin + SLOTS]
        same = (seg_pad[:, begin:begin + SLOTS] == segment).astype(gated_linear_unit.dtype)
        total = total + kernel[offset] * piece * same[:, :, None]
    return total

def convolve(values, gain, w_in, kernel, bn_gain, bn_bias, w_out, segment, valid_frames):
    entry_value = low(layer_norm(values, gain))
    joint_projection = low_back(matmul(entry_value, w_in))
    gated_linear_unit = joint_projection[:, :D] * jax.nn.sigmoid(joint_projection[:, D:]) * valid_frames[:, None]
    mixed_rows = jax.checkpoint(depthwise)(gated_linear_unit.reshape(DEVICES, SLOTS, D), segment, kernel).reshape(DEVICES * SLOTS, D)
    frame_count = jnp.sum(valid_frames)
    centered_rows = lax.optimization_barrier(jnp.sum(mixed_rows * valid_frames[:, None], axis=0)) / frame_count
    square = lax.optimization_barrier(jnp.sum(mixed_rows * mixed_rows * valid_frames[:, None], axis=0)) / frame_count
    inverse_deviation = lax.rsqrt(square - centered_rows * centered_rows + EPS)
    normed = (mixed_rows - centered_rows) * inverse_deviation * bn_gain + bn_bias
    activation_value = low(swish(normed))
    return low_back(matmul(activation_value, w_out))

def forward(params, inputs, lengths, mask):
    first_norm, first_up, first_down, attend_norm, attend_joint, attend_out, conv_norm, conv_in, conv_kernel, batch_gain, batch_bias, conv_out, second_norm, second_up, second_down, final_norm = params
    results = []
    for micro in range(MB):
        segment, position = jax.vmap(frame_layout)(lengths[micro])
        valid_frames = mask[micro].astype(inputs.dtype)
        state = inputs[micro]
        state = state + 0.5 * feed(state, first_norm, first_up, first_down)
        state = state + attention(state, attend_norm, attend_joint, attend_out, segment, position, valid_frames)
        state = state + convolve(state, conv_norm, conv_in, conv_kernel, batch_gain, batch_bias, conv_out, segment, valid_frames)
        state = state + 0.5 * feed(state, second_norm, second_up, second_down)
        results.append(layer_norm(state, final_norm))
    return jnp.stack(results)

def reference(frames, item_lengths, frame_mask, first_norm, first_up, first_down, attend_norm, attend_joint, attend_out, conv_norm, conv_in, conv_kernel, batch_gain, batch_bias, conv_out, second_norm, second_up, second_down, final_norm, output_grad):
    params = tuple((weight.astype(jnp.float32) for weight in (first_norm, first_up, first_down, attend_norm, attend_joint, attend_out, conv_norm, conv_in, conv_kernel, batch_gain, batch_bias, conv_out, second_norm, second_up, second_down, final_norm)))

    def run(weights, inputs):
        return forward(weights, inputs, item_lengths, frame_mask)
    result, pullback = jax.vjp(run, params, frames.astype(jnp.float32))
    grads, input_grad = pullback(output_grad.astype(jnp.float32))
    return (result.astype(jnp.bfloat16), input_grad.astype(jnp.bfloat16), grads[0], grads[1], grads[2], grads[3], grads[4], grads[5], grads[6], grads[7], grads[8], grads[9], grads[10], grads[11], grads[12], grads[13], grads[14], grads[15])
```

```python
import functools
import math

import jax
import jax.numpy as jnp
from jax import lax
from jax.sharding import PartitionSpec as P

HEADS = 8
KER = 32
HDIM = 64
MB = 2


EPS = 1e-05

def swap(value, axis, bit, size):
    return lax.ppermute(value, axis, [(i, i ^ bit) for i in range(size)])


def bits_of(size):
    return [1 << i for i in range(size.bit_length() - 1)]


def sum_all(value, sizes):
    for bit in bits_of(sizes["dp"]):
        value = value + swap(value, "dp", bit, sizes["dp"])
    return value + swap(value, "fsdp", 1, 2)


def gather_shard(shard):
    other = swap(shard, "fsdp", 1, 2)
    first = lax.axis_index("fsdp") == 0
    return jnp.concatenate([jnp.where(first, shard, other), jnp.where(first, other, shard)], axis=0)


def split_half(value, index):
    half = value.shape[0] // 2
    keep = lax.dynamic_slice_in_dim(value, index * half, half, axis=0)
    send = lax.dynamic_slice_in_dim(value, (1 - index) * half, half, axis=0)
    return keep, send


def reduce_rows(value, sizes):
    f32 = jnp.float32
    dp = lax.axis_index("dp")
    core, x = dp & 1, lax.axis_index("fsdp")
    keep = lax.dynamic_index_in_dim(value, core, 1, keepdims=False)
    send = lax.dynamic_index_in_dim(value, 1 - core, 1, keepdims=False)
    got = swap(send, "dp", 1, sizes["dp"])
    keep = (keep.astype(f32) + got.astype(f32)).astype(jnp.bfloat16)
    keep, send = split_half(keep, x)
    keep, send = keep[0], send[0]
    got = swap(send, "fsdp", 1, 2)
    keep = (keep.astype(f32) + got.astype(f32)).astype(jnp.bfloat16)
    bits = bits_of(sizes["dp"])[1:]
    for bit in bits:
        index = ((dp & bit) > 0).astype(jnp.int32)
        keep, send = split_half(keep, index)
        got = swap(send, "dp", bit, sizes["dp"])
        keep = (keep.astype(f32) + got.astype(f32)).astype(jnp.bfloat16)
    for bit in bits[::-1] + [1]:
        low = (dp & bit) == 0
        got = swap(keep, "dp", bit, sizes["dp"])
        keep = jnp.concatenate([jnp.where(low, keep, got), jnp.where(low, got, keep)], axis=0)
    return keep.reshape(2, -1, 512)


def product(left, right):
    return jnp.dot(left, right, preferred_element_type=jnp.float32)


def product_tn(left, right):
    return lax.dot_general(
        left, right, (((0,), (0,)), ((), ())), preferred_element_type=jnp.float32
    )


def product_nt(left, right):
    return lax.dot_general(
        left, right, (((1,), (1,)), ((), ())), preferred_element_type=jnp.float32
    )


def normalize(values, gain):
    centered = values - jnp.mean(values, axis=-1, keepdims=True)
    inverse_deviation = lax.rsqrt(jnp.mean(centered * centered, axis=-1, keepdims=True) + EPS)
    normal_rows = centered * inverse_deviation
    return (normal_rows * gain, normal_rows, inverse_deviation)


def normalize_back(grad_out, normal_rows, inverse_deviation, gain):
    scaled = grad_out * gain
    grad_in = inverse_deviation * (
        scaled
        - jnp.mean(scaled, axis=-1, keepdims=True)
        - normal_rows * jnp.mean(scaled * normal_rows, axis=-1, keepdims=True)
    )
    return (grad_in, jnp.sum(grad_out * normal_rows, axis=0))


def swish_grad(values):
    gate_sigmoid = jax.nn.sigmoid(values)
    return gate_sigmoid * (1.0 + values * (1.0 - gate_sigmoid))


def frame_layout(lengths, slots):
    ends = jnp.cumsum(lengths)
    starts = ends - lengths
    slot_ids = jnp.arange(slots, dtype=jnp.int32)
    segment = jnp.sum((slot_ids[:, None] >= ends[None, :]).astype(jnp.int32), axis=1)
    member = segment[:, None] == jnp.arange(lengths.shape[0], dtype=jnp.int32)[None, :]
    begin = jnp.sum(jnp.where(member, starts[None, :], 0), axis=1)
    return (segment, slot_ids - begin)


def rotate(values, position, sign):
    half = HDIM // 2
    freq = jnp.exp(jnp.arange(half, dtype=jnp.float32) * (-2.0 * math.log(10000.0) / HDIM))
    angle = position.astype(jnp.float32)[:, None] * freq[None, :]
    cosine = jnp.cos(angle)[:, None, :]
    sine = sign * jnp.sin(angle)[:, None, :]
    first = values[..., :half]
    second = values[..., half:]
    return jnp.concatenate(
        [first * cosine - second * sine, first * sine + second * cosine], axis=-1
    )


def shifted(array, shift_by, fill):
    length = array.shape[0]
    pad_width = ((KER, KER),) + ((0, 0),) * (array.ndim - 1)
    padded = jnp.pad(array, pad_width, constant_values=fill)
    return lax.slice_in_dim(padded, KER + shift_by, KER + shift_by + length, axis=0)


def feed_forward(values, gain, w_up, w_down):
    normed, normal_rows, inverse_deviation = normalize(values, gain)
    entry_value = normed.astype(jnp.bfloat16)
    inner = product(entry_value, w_up)
    hidden = (inner * jax.nn.sigmoid(inner)).astype(jnp.bfloat16)
    return (product(hidden, w_down), (entry_value, normal_rows, inverse_deviation, inner, hidden))


def feed_back(grad_state, gain, w_up, w_down, saved_tensors):
    entry_value, normal_rows, inverse_deviation, inner, hidden = saved_tensors
    grad_branch = (0.5 * grad_state).astype(jnp.bfloat16)
    grad_down = product_tn(hidden, grad_branch)
    grad_hidden = product_nt(grad_branch, w_down)
    grad_inner = (grad_hidden * swish_grad(inner)).astype(jnp.bfloat16)
    grad_up = product_tn(entry_value, grad_inner)
    grad_entry = product_nt(grad_inner, w_up)
    grad_input, grad_gain = normalize_back(grad_entry, normal_rows, inverse_deviation, gain)
    return (grad_state + grad_input, (grad_gain, grad_up, grad_down))


def block_scores(query, keys, segment, valid_frames, row_start, block_rows):
    scores = jnp.einsum("qhd,khd->hqk", query, keys, preferred_element_type=jnp.float32)
    row_ids = jnp.arange(block_rows, dtype=jnp.int32) + row_start
    col_ids = jnp.arange(keys.shape[0], dtype=jnp.int32)
    allowed = (segment[row_start : row_start + block_rows, None] == segment[None, :]) & (
        (valid_frames[None, :] > 0) | (row_ids[:, None] == col_ids[None, :])
    )
    return jnp.where(allowed[None, :, :], scores, -1000000000.0)


def attention(values, gain, w_joint, w_out, segment, position, valid_frames):
    normed, normal_rows, inverse_deviation = normalize(values, gain)
    entry_value = normed.astype(jnp.bfloat16)
    slots = values.shape[0]
    joint_projection = product(entry_value, w_joint).reshape(slots, 3, HEADS, HDIM)
    query = (rotate(joint_projection[:, 0], position, 1.0) * HDIM ** (-0.5)).astype(jnp.bfloat16)
    keys = rotate(joint_projection[:, 1], position, 1.0).astype(jnp.bfloat16)
    vals = joint_projection[:, 2].astype(jnp.bfloat16)
    block_rows = min(512, slots)
    scores = block_scores(query, keys, segment, valid_frames, 0, block_rows)
    row_max = jnp.max(scores, axis=-1, keepdims=True)
    expo = jnp.exp(scores - row_max)
    row_sum = jnp.sum(expo, axis=-1, keepdims=True)
    probs = (expo / row_sum).astype(jnp.bfloat16)
    outputs = jnp.einsum("hqk,khd->qhd", probs, vals, preferred_element_type=jnp.float32).astype(
        jnp.bfloat16
    )
    totals = row_max + jnp.log(row_sum)
    mixed_rows = outputs.reshape(slots, HEADS * HDIM)
    return (
        product(mixed_rows, w_out),
        (entry_value, normal_rows, inverse_deviation, query, keys, vals, totals, mixed_rows),
    )


def attend_back(grad_state, gain, w_joint, w_out, segment, position, valid_frames, saved_tensors):
    entry_value, normal_rows, inverse_deviation, query, keys, vals, log_total, mixed_rows = (
        saved_tensors
    )
    slots = grad_state.shape[0]
    grad_branch = grad_state.astype(jnp.bfloat16)
    grad_out = product_tn(mixed_rows, grad_branch)
    grad_mixed = product_nt(grad_branch, w_out).astype(jnp.bfloat16).reshape(slots, HEADS, HDIM)
    block_rows = min(512, slots)
    scores = block_scores(query, keys, segment, valid_frames, 0, block_rows)
    probs = jnp.exp(scores - log_total)
    grad_probs = jnp.einsum("qhd,khd->hqk", grad_mixed, vals, preferred_element_type=jnp.float32)
    grad_scores = (
        probs * (grad_probs - jnp.sum(probs * grad_probs, axis=-1, keepdims=True))
    ).astype(jnp.bfloat16)
    query_parts = jnp.einsum("hqk,khd->qhd", grad_scores, keys, preferred_element_type=jnp.float32)
    grad_keys = jnp.einsum("hqk,qhd->khd", grad_scores, query, preferred_element_type=jnp.float32)
    grad_vals = jnp.einsum(
        "hqk,qhd->khd", probs.astype(jnp.bfloat16), grad_mixed, preferred_element_type=jnp.float32
    )
    grad_query = rotate(query_parts * HDIM ** (-0.5), position, -1.0)
    grad_keys = rotate(grad_keys, position, -1.0)
    grad_joint = jnp.stack([grad_query, grad_keys, grad_vals], axis=1).reshape(
        slots, 3 * HEADS * HDIM
    )
    grad_joint = grad_joint.astype(jnp.bfloat16)
    grad_w_joint = product_tn(entry_value, grad_joint)
    grad_entry = product_nt(grad_joint, w_joint)
    grad_input, grad_gain = normalize_back(grad_entry, normal_rows, inverse_deviation, gain)
    return (grad_state + grad_input, (grad_gain, grad_w_joint, grad_out))


def conv_forward(
    values, gain, w_in, kernel, batch_gain_part, batch_bias_part, w_out, segment, valid_frames, sizes
):
    normed, normal_rows, inverse_deviation = normalize(values, gain)
    entry_value = normed.astype(jnp.bfloat16)
    joint_projection = product(entry_value, w_in)
    width = joint_projection.shape[1] // 2
    gate_sigmoid = jax.nn.sigmoid(joint_projection[:, width:])
    gated_linear_unit = joint_projection[:, :width] * gate_sigmoid * valid_frames[:, None]
    mixed_rows = jnp.zeros(gated_linear_unit.shape, jnp.float32)
    for offset in range(KER):
        shift_by = offset - (KER - 1) // 2
        same = (shifted(segment, shift_by, -1) == segment).astype(jnp.float32)[:, None]
        mixed_rows = mixed_rows + kernel[offset] * shifted(gated_linear_unit, shift_by, 0.0) * same
    local_sums = (
        jnp.sum(mixed_rows * valid_frames[:, None], axis=0),
        jnp.sum(mixed_rows * mixed_rows * valid_frames[:, None], axis=0),
        jnp.sum(valid_frames),
    )
    packed = jnp.stack([local_sums[0], local_sums[1], jnp.full_like(local_sums[0], local_sums[2])])
    sum_first, sum_second, frame_count = sum_all(packed, sizes)
    centered_rows = sum_first / frame_count
    batch_inverse_std = lax.rsqrt(sum_second / frame_count - centered_rows * centered_rows + EPS)
    normalized_input = (mixed_rows - centered_rows) * batch_inverse_std
    batch_normed_rows = normalized_input * batch_gain_part + batch_bias_part
    activation_value = (batch_normed_rows * jax.nn.sigmoid(batch_normed_rows)).astype(jnp.bfloat16)
    saved_tensors = (
        entry_value,
        normal_rows,
        inverse_deviation,
        joint_projection,
        gate_sigmoid,
        gated_linear_unit,
        normalized_input,
        batch_inverse_std,
        batch_normed_rows,
        activation_value,
        frame_count,
    )
    return (product(activation_value, w_out), saved_tensors)


def conv_back(
    grad_state, gain, w_in, kernel, batch_gain_part, w_out, segment, valid_frames, saved_tensors, sizes
):
    (
        entry_value,
        normal_rows,
        inverse_deviation,
        joint_projection,
        gate_sigmoid,
        gated_linear_unit,
        normalized_input,
        batch_inverse_std,
        batch_normed_rows,
        activation_value,
        frame_count,
    ) = saved_tensors
    grad_branch = grad_state.astype(jnp.bfloat16)
    grad_w_out = product_tn(activation_value, grad_branch)
    batch_gradient = product_nt(grad_branch, w_out) * swish_grad(batch_normed_rows)
    local_bias = jnp.sum(batch_gradient, axis=0)
    local_gain_sum = jnp.sum(batch_gradient * normalized_input, axis=0)
    summed_bias_gradient, summed_gain_gradient = sum_all(
        jnp.stack([local_bias, local_gain_sum]), sizes
    )
    grad_mixed = batch_inverse_std * (
        batch_gradient * batch_gain_part
        - valid_frames[:, None]
        / frame_count
        * (
            batch_gain_part * summed_bias_gradient
            + normalized_input * batch_gain_part * summed_gain_gradient
        )
    )
    grad_glu = jnp.zeros(gated_linear_unit.shape, jnp.float32)
    kernel_rows = []
    for offset in range(KER):
        shift_by = offset - (KER - 1) // 2
        same_fwd = (shifted(segment, shift_by, -1) == segment).astype(jnp.float32)[:, None]
        kernel_rows.append(
            jnp.sum(grad_mixed * shifted(gated_linear_unit, shift_by, 0.0) * same_fwd, axis=0)
        )
        same_back = (shifted(segment, -shift_by, -1) == segment).astype(jnp.float32)[:, None]
        grad_glu = grad_glu + kernel[offset] * shifted(grad_mixed, -shift_by, 0.0) * same_back
    grad_glu = grad_glu * valid_frames[:, None]
    width = joint_projection.shape[1] // 2
    grad_joint = jnp.concatenate(
        [
            grad_glu * gate_sigmoid,
            grad_glu * joint_projection[:, :width] * gate_sigmoid * (1.0 - gate_sigmoid),
        ],
        axis=1,
    )
    grad_joint = grad_joint.astype(jnp.bfloat16)
    grad_w_in = product_tn(entry_value, grad_joint)
    grad_entry = product_nt(grad_joint, w_in)
    grad_input, grad_gain = normalize_back(grad_entry, normal_rows, inverse_deviation, gain)
    grads = (grad_gain, grad_w_in, jnp.stack(kernel_rows), local_gain_sum, local_bias, grad_w_out)
    return (grad_state + grad_input, grads)


def collect(shards):
    return tuple(gather_shard(shard) for shard in shards)


def add_tuples(first_set, second_set):
    return tuple((left_item + right_item for left_item, right_item in zip(first_set, second_set)))


def body(
    sizes,
    frames,
    item_lengths,
    frame_mask,
    first_norm,
    first_up,
    first_down,
    attend_norm,
    attend_joint,
    attend_out,
    conv_norm,
    conv_in,
    conv_kernel,
    batch_gain,
    batch_bias,
    conv_out,
    second_norm,
    second_up,
    second_down,
    final_norm,
    output_grad,
):
    shards = (
        first_norm,
        first_up,
        first_down,
        attend_norm,
        attend_joint,
        attend_out,
        conv_norm,
        conv_in,
        conv_kernel,
        batch_gain,
        batch_bias,
        conv_out,
        second_norm,
        second_up,
        second_down,
        final_norm,
    )
    slots = frames.shape[1]
    parts = None
    full = collect(shards)
    outputs = []
    input_grads = []
    for micro in range(MB):
        (
            norm_one,
            up_one,
            down_one,
            norm_attend,
            joint_attend,
            out_attend,
            norm_conv,
            in_conv,
            kernel_conv,
            batch_gain_part,
            batch_bias_part,
            out_conv,
            norm_two,
            up_two,
            down_two,
            norm_last,
        ) = full
        segment, position = frame_layout(item_lengths[micro, 0], slots)
        valid_frames = frame_mask[micro].astype(jnp.float32)
        entered = frames[micro].astype(jnp.float32)
        branch, saved_one = feed_forward(entered, norm_one.astype(jnp.float32), up_one, down_one)
        after_one = entered + 0.5 * branch
        branch, saved_attend = attention(
            after_one,
            norm_attend.astype(jnp.float32),
            joint_attend,
            out_attend,
            segment,
            position,
            valid_frames,
        )
        after_attend = after_one + branch
        branch, saved_conv = conv_forward(
            after_attend,
            norm_conv.astype(jnp.float32),
            in_conv,
            kernel_conv.astype(jnp.float32),
            batch_gain_part.astype(jnp.float32),
            batch_bias_part.astype(jnp.float32),
            out_conv,
            segment,
            valid_frames,
            sizes,
        )
        after_conv = after_attend + branch
        branch, saved_two = feed_forward(after_conv, norm_two.astype(jnp.float32), up_two, down_two)
        after_two = after_conv + 0.5 * branch
        final_out, final_normal, final_inv = normalize(after_two, norm_last.astype(jnp.float32))
        outputs.append(final_out.astype(jnp.bfloat16))
        grad_state, grad_last = normalize_back(
            output_grad[micro].astype(jnp.float32),
            final_normal,
            final_inv,
            norm_last.astype(jnp.float32),
        )
        grad_state, grads_two = feed_back(
            grad_state, norm_two.astype(jnp.float32), up_two, down_two, saved_two
        )
        grad_state, grads_conv = conv_back(
            grad_state,
            norm_conv.astype(jnp.float32),
            in_conv,
            kernel_conv.astype(jnp.float32),
            batch_gain_part.astype(jnp.float32),
            out_conv,
            segment,
            valid_frames,
            saved_conv,
            sizes,
        )
        grad_state, grads_attend = attend_back(
            grad_state,
            norm_attend.astype(jnp.float32),
            joint_attend,
            out_attend,
            segment,
            position,
            valid_frames,
            saved_attend,
        )
        grad_state, grads_one = feed_back(
            grad_state, norm_one.astype(jnp.float32), up_one, down_one, saved_one
        )
        input_grads.append(grad_state.astype(jnp.bfloat16))
        grads = (
            grads_one[0],
            grads_one[1],
            grads_one[2],
            grads_attend[0],
            grads_attend[1],
            grads_attend[2],
            grads_conv[0],
            grads_conv[1],
            grads_conv[2],
            grads_conv[3],
            grads_conv[4],
            grads_conv[5],
            grads_two[0],
            grads_two[1],
            grads_two[2],
            grad_last,
        )
        parts = grads if parts is None else add_tuples(parts, grads)
    big = [1, 2, 4, 5, 7, 11, 13, 14]
    small = [i for i in range(16) if i not in big]
    packed = jnp.concatenate(
        [parts[i].astype(jnp.bfloat16).reshape(2, 2, -1, 512) for i in big], axis=2
    )
    reduced = reduce_rows(packed, sizes).astype(jnp.float32)
    totals = [None] * 16
    at = 0
    for i in big:
        rows, columns = parts[i].shape
        count = rows * columns // 2048
        totals[i] = reduced[:, at : at + count].reshape(rows // 2, columns)
        at += count
    flat = sum_all(jnp.concatenate([parts[i].reshape(-1, 512) for i in small], axis=0), sizes)
    at = 0
    for i in small:
        count = parts[i].size // 512
        whole = flat[at : at + count].reshape(parts[i].shape)
        half = parts[i].shape[0] // 2
        totals[i] = lax.dynamic_slice_in_dim(whole, lax.axis_index("fsdp") * half, half, axis=0)
        at += count
    return (
        jnp.stack(outputs),
        jnp.stack(input_grads),
        totals[0],
        totals[1],
        totals[2],
        totals[3],
        totals[4],
        totals[5],
        totals[6],
        totals[7],
        totals[8],
        totals[9],
        totals[10],
        totals[11],
        totals[12],
        totals[13],
        totals[14],
        totals[15],
    )


def solution(mesh):
    sizes = dict(mesh.shape)
    return jax.shard_map(
        functools.partial(body, sizes),
        mesh=mesh,
        in_specs=(
            P(None, ("dp", "fsdp"), None),
            P(None, ("dp", "fsdp"), None),
            P(None, ("dp", "fsdp")),
            P("fsdp"),
            P("fsdp", None),
            P("fsdp", None),
            P("fsdp"),
            P("fsdp", None),
            P("fsdp", None),
            P("fsdp"),
            P("fsdp", None),
            P("fsdp", None),
            P("fsdp"),
            P("fsdp"),
            P("fsdp", None),
            P("fsdp"),
            P("fsdp", None),
            P("fsdp", None),
            P("fsdp"),
            P(None, ("dp", "fsdp"), None),
        ),
        out_specs=(
            P(None, ("dp", "fsdp"), None),
            P(None, ("dp", "fsdp"), None),
            P("fsdp"),
            P("fsdp", None),
            P("fsdp", None),
            P("fsdp"),
            P("fsdp", None),
            P("fsdp", None),
            P("fsdp"),
            P("fsdp", None),
            P("fsdp", None),
            P("fsdp"),
            P("fsdp"),
            P("fsdp", None),
            P("fsdp"),
            P("fsdp", None),
            P("fsdp", None),
            P("fsdp"),
        ),
        check_vma=False,
    )
```

```python
import functools
import math

import jax
import jax.numpy as jnp
from jax import lax
from jax.experimental import pallas as pl
from jax.experimental.pallas import tpu as pltpu
from jax.sharding import PartitionSpec as P

HEADS = 8
KER = 32
HDIM = 64
MB = 2
D = 512
FF = 2048
EPS = 1e-05
PAD = 16
F32 = jnp.float32
BF16 = jnp.bfloat16
ANY = pl.BlockSpec(memory_space=pl.ANY)
SMEM = pl.BlockSpec(memory_space=pltpu.SMEM)


def swap(value, axis, bit, size):
    return lax.ppermute(value, axis, [(i, i ^ bit) for i in range(size)])


def bits_of(size):
    return [1 << i for i in range(size.bit_length() - 1)]


def sum_all(value, sizes):
    for bit in bits_of(sizes["dp"]):
        value = value + swap(value, "dp", bit, sizes["dp"])
    return value + swap(value, "fsdp", 1, 2)


def add_split(keep, got, index):
    half = keep.shape[0] // 2
    parts = []
    for at in (index, 1 - index):
        left = lax.dynamic_slice_in_dim(keep, at * half, half, axis=0)
        right = lax.dynamic_slice_in_dim(got, at * half, half, axis=0)
        parts.append((left.astype(F32) + right.astype(F32)).astype(BF16))
    return parts


def reduce_rows(send, keep, sizes):
    dp = lax.axis_index("dp")
    got = swap(send, "dp", 1, sizes["dp"])
    keep, send = add_split(keep, got, lax.axis_index("fsdp"))
    keep, send = keep[0], send[0]
    got = swap(send, "fsdp", 1, 2)
    bits = bits_of(sizes["dp"])[1:]
    for bit in bits:
        keep, send = add_split(keep, got, ((dp & bit) > 0).astype(jnp.int32))
        got = swap(send, "dp", bit, sizes["dp"])
    keep = (keep.astype(F32) + got.astype(F32)).astype(BF16)
    for bit in bits[::-1] + [1]:
        low = (dp & bit) == 0
        got = swap(keep, "dp", bit, sizes["dp"])
        keep = jnp.concatenate([jnp.where(low, keep, got), jnp.where(low, got, keep)], axis=0)
    return keep.reshape(2, -1, D)


def dot(left, right):
    return lax.dot_general(left, right, (((1,), (0,)), ((), ())), preferred_element_type=F32)


def dot_nt(left, right):
    return lax.dot_general(left, right, (((1,), (1,)), ((), ())), preferred_element_type=F32)


def dot_tn(left, right):
    return lax.dot_general(left, right, (((0,), (0,)), ((), ())), preferred_element_type=F32)


def sigmoid(values):
    return 0.5 * jnp.tanh(0.5 * values) + 0.5


def norm(values):
    centered = values - jnp.mean(values, axis=-1, keepdims=True)
    inverse = lax.rsqrt(jnp.mean(centered * centered, axis=-1, keepdims=True) + EPS)
    return centered * inverse, inverse


def norm_back(grad, rows, inverse, gain):
    scaled = grad * gain
    return inverse * (
        scaled
        - jnp.mean(scaled, axis=-1, keepdims=True)
        - rows * jnp.mean(scaled * rows, axis=-1, keepdims=True)
    )


def column_sum(values):
    return jnp.sum(values, axis=0, keepdims=True)


def fetch(index, sources, targets, sem):
    copies = []
    for i, (mine, other) in enumerate(sources):
        rows = mine.shape[0]
        for j, source in enumerate((mine, other)):
            at = pl.multiple_of((index if j == 0 else 1 - index) * rows, rows)
            copies.append(
                pltpu.make_async_copy(source, targets[i].at[pl.ds(at, rows)], sem.at[2 * i + j])
            )
    for copy in copies:
        copy.start()
    for copy in copies:
        copy.wait()


def weight_scratch(*shapes):
    return [pltpu.VMEM(shape, BF16) for shape in shapes] + [
        pltpu.SemaphoreType.DMA((2 * len(shapes),))
    ]


def tile4(values):
    return jnp.concatenate([values] * 4, axis=1)


def turn(values, cosine, sine):
    lane = lax.broadcasted_iota(jnp.int32, (values.shape[0], 128), 1)
    first = (lane & 63) < 32
    parts = []
    for c in range(4):
        u = values[:, c * 128 : (c + 1) * 128]
        swapped = jnp.where(first, pltpu.roll(u, 96, 1), pltpu.roll(u, 32, 1))
        parts.append(u * cosine + swapped * sine)
    return jnp.concatenate(parts, axis=1)


def head_masks():
    lane = lax.broadcasted_iota(jnp.int32, (1, 128), 1)
    return [((lane >> 6) == e).astype(F32).astype(BF16) for e in range(2)]


def feed_kernel(idx, x, gain, um, uo, dm, do, x1, a1, h1, g1, u, d, sem):
    @pl.when(pl.program_id(0) == 0)
    def _():
        fetch(idx[0], ((um, uo), (dm, do)), (u, d), sem)

    v = x[...].astype(F32)
    a = (norm(v)[0] * gain[...]).astype(BF16)
    a1[...] = a
    acc = None
    for j in range(4):
        c = slice(j * 512, (j + 1) * 512)
        z = dot(a, u[:, c])
        s = sigmoid(z)
        h = z * s
        g1[:, c] = (s + h * (1.0 - s)).astype(BF16)
        h = h.astype(BF16)
        h1[:, c] = h
        part = dot(h, d[c, :])
        acc = part if acc is None else acc + part
    x1[...] = v + 0.5 * acc


def attend_kernel(
    idx, x1, gain, cos, sin, segb, rows, jm, jo, om, oo,
    x2, a2, qo, ko, vo, pr, mixed, wj, wo, bias, sem,
):
    @pl.when(pl.program_id(0) == 0)
    def _():
        fetch(idx[0], ((jm, jo), (om, oo)), (wj, wo), sem)

    v = x1[0]
    a = (norm(v)[0] * gain[...]).astype(BF16)
    a2[0] = a
    cosine, sine = cos[0], sin[0]
    qo[0] = (turn(dot(a, wj[:, :512]), cosine, sine) * HDIM ** (-0.5)).astype(BF16)
    ko[0] = turn(dot(a, wj[:, 512:1024]), cosine, sine).astype(BF16)
    vo[0] = dot(a, wj[:, 1024:]).astype(BF16)
    size = bias.shape[0]
    row = lax.broadcasted_iota(jnp.int32, (size, size), 0)
    col = lax.broadcasted_iota(jnp.int32, (size, size), 1)
    allowed = (tile4(segb[0]) == rows[0, 0:1, :]) & ((rows[0, 1:2, :] > 0) | (row == col))
    bias[...] = jnp.where(allowed, 0.0, -1000000000.0)
    masks = head_masks()

    def pair(p, carry):
        c = pl.ds(pl.multiple_of(p * 128, 128), 128)
        q, k, val = qo[0, :, c], ko[0, :, c], vo[0, :, c]
        total = None
        for e in range(2):
            s = dot_nt(q * masks[e], k) + bias[...]
            ex = jnp.exp(s - jnp.max(s, axis=-1, keepdims=True))
            prob = (ex / jnp.sum(ex, axis=-1, keepdims=True)).astype(BF16)
            pr[0, 2 * p + e] = prob
            part = dot(prob, val * masks[e])
            total = part if total is None else total + part
        mixed[0, :, c] = total.astype(BF16)
        return carry

    lax.fori_loop(0, HEADS // 2, pair, 0)
    x2[0] = v + dot(mixed[0], wo[...])


def conv_taps(padded, shifts, fill):
    rows = shifts.shape[1]
    for b in range(8):
        shifts[b] = padded[b : b + rows, :]


def conv_kernel(
    idx, x2, gain, kern, validb, before, after, wm, wo,
    a3, glu, p1, p2, cout, stats, w, padded, shifts, sem,
):
    fetch(idx[0], ((wm, wo),), (w,), sem)
    a = (norm(x2[0])[0] * gain[...]).astype(BF16)
    a3[...] = a
    valid = tile4(validb[0])
    g1 = dot(a, w[:, :512])
    s = sigmoid(dot(a, w[:, 512:])) * valid
    g = g1 * s
    glu[...] = g
    p1[...] = s.astype(BF16)
    p2[...] = (g * (1.0 - s)).astype(BF16)
    size = g.shape[0]
    padded[0:PAD] = jnp.zeros((PAD, D), F32)
    padded[PAD : PAD + size] = g
    padded[PAD + size :] = jnp.zeros((padded.shape[0] - PAD - size, D), F32)
    conv_taps(padded, shifts, 0)
    chunk = 32

    def step(i, carry):
        r0 = pl.multiple_of(i * chunk, chunk)
        low, high = before[0, pl.ds(r0, chunk), :], after[0, pl.ds(r0, chunk), :]
        acc = [jnp.zeros((chunk, 128), F32) for _ in range(4)]
        for o in range(KER):
            shift_by = o - (KER - 1) // 2
            a8, b = divmod(shift_by + PAD, 8)
            if shift_by < 0:
                keep = low >= float(-shift_by)
            elif shift_by > 0:
                keep = high >= float(shift_by)
            for c in range(4):
                cs = slice(c * 128, (c + 1) * 128)
                value = shifts[b, pl.ds(r0 + 8 * a8, chunk), cs]
                if shift_by != 0:
                    value = jnp.where(keep, value, 0.0)
                acc[c] = acc[c] + kern[o : o + 1, cs] * value
        for c in range(4):
            cout[pl.ds(r0, chunk), c * 128 : (c + 1) * 128] = acc[c]
        return carry

    lax.fori_loop(0, size // chunk, step, 0)
    out = cout[...]
    weighted = out * valid
    stats[0:1] = column_sum(weighted)
    stats[1:2] = column_sum(weighted * out)
    stats[2:3] = column_sum(valid)
    stats[3:8] = jnp.zeros((5, D), F32)


def middle_kernel(
    idx, total, gains, conv, x2, og, cm, co, um, uo, dm, do,
    enc, a4, e3, a5, h2, dz, e4, db, dx3, sums, wc, u, d, deriv, sem,
):
    @pl.when(pl.program_id(0) == 0)
    def _():
        fetch(idx[0], ((cm, co), (um, uo), (dm, do)), (wc, u, d), sem)
        sums[...] = jnp.zeros(sums.shape, F32)

    gain_b, bias_b, gain_2, gain_f = (gains[i : i + 1] for i in range(4))
    count = total[2:3]
    mean = total[0:1] / count
    inverse = lax.rsqrt(total[1:2] / count - mean * mean + EPS)
    unit = (conv[...] - mean) * inverse
    act = unit * gain_b + bias_b
    s_act = sigmoid(act)
    a = (act * s_act).astype(BF16)
    a4[...] = a
    v3 = x2[0] + dot(a, wc[...])
    n5, inv5 = norm(v3)
    a = (n5 * gain_2).astype(BF16)
    a5[...] = a
    acc = None
    for j in range(4):
        c = slice(j * 512, (j + 1) * 512)
        z = dot(a, u[:, c])
        s = sigmoid(z)
        h = z * s
        deriv[:, c] = (s + h * (1.0 - s)).astype(BF16)
        h = h.astype(BF16)
        h2[:, c] = h
        part = dot(h, d[c, :])
        acc = part if acc is None else acc + part
    n6, inv6 = norm(v3 + 0.5 * acc)
    enc[...] = (n6 * gain_f).astype(BF16)
    dy = og[0].astype(F32)
    sums[3:4] += column_sum(dy * n6)
    grad4 = norm_back(dy, n6, inv6, gain_f)
    e = (0.5 * grad4).astype(BF16)
    e4[...] = e
    acc = None
    for j in range(4):
        c = slice(j * 512, (j + 1) * 512)
        g = (dot_nt(e, d[c, :]) * deriv[:, c].astype(F32)).astype(BF16)
        dz[:, c] = g
        part = dot_nt(g, u[:, c])
        acc = part if acc is None else acc + part
    sums[2:3] += column_sum(acc * n5)
    grad3 = grad4 + norm_back(acc, n5, inv5, gain_2)
    dx3[...] = grad3
    e = grad3.astype(BF16)
    e3[...] = e
    dact = dot_nt(e, wc[...]) * (s_act * (1.0 + act * (1.0 - s_act)))
    db[...] = dact
    sums[0:1] += column_sum(dact)
    sums[1:2] += column_sum(dact * unit)


def conv_back_kernel(
    idx, total, back, gains, kern, conv, db, glu, p1, p2, x2, dx3, validb, before, after, wm, wo,
    dg, dx2, e2, dk, sums, w, padded, shifts, dglu, dkacc, sem,
):
    fetch(idx[0], ((wm, wo),), (w,), sem)
    gain_b, gain_c = gains[0:1], gains[1:2]
    count = total[2:3]
    mean = total[0:1] / count
    inverse = lax.rsqrt(total[1:2] / count - mean * mean + EPS)
    valid = tile4(validb[0])
    unit = (conv[...] - mean) * inverse
    dc = inverse * (
        db[...] * gain_b - valid / count * (gain_b * back[0:1] + unit * (gain_b * back[1:2]))
    )
    size = dc.shape[0]
    padded[0:PAD] = jnp.zeros((PAD, D), F32)
    padded[PAD : PAD + size] = dc
    padded[PAD + size :] = jnp.zeros((padded.shape[0] - PAD - size, D), F32)
    conv_taps(padded, shifts, 0)
    dkacc[...] = jnp.zeros(dkacc.shape, F32)
    chunk = 32

    def step(i, carry):
        r0 = pl.multiple_of(i * chunk, chunk)
        low, high = before[0, pl.ds(r0, chunk), :], after[0, pl.ds(r0, chunk), :]
        for c in range(4):
            cs = slice(c * 128, (c + 1) * 128)
            own = glu[pl.ds(r0, chunk), cs]
            acc = jnp.zeros((chunk, 128), F32)
            for o in range(KER):
                shift_by = (KER - 1) // 2 - o
                a8, b = divmod(shift_by + PAD, 8)
                value = shifts[b, pl.ds(r0 + 8 * a8, chunk), cs]
                if shift_by < 0:
                    value = jnp.where(low >= float(-shift_by), value, 0.0)
                elif shift_by > 0:
                    value = jnp.where(high >= float(shift_by), value, 0.0)
                acc = acc + kern[o : o + 1, cs] * value
                prod = own * value
                part = prod[0:8]
                for q in range(1, chunk // 8):
                    part = part + prod[8 * q : 8 * q + 8]
                dkacc[o, :, cs] += part
            dglu[pl.ds(r0, chunk), cs] = acc
        return carry

    lax.fori_loop(0, size // chunk, step, 0)
    dk[...] = jnp.sum(dkacc[...], axis=1)
    grad = dglu[...]
    g1 = (grad * p1[...].astype(F32)).astype(BF16)
    g2 = (grad * p2[...].astype(F32)).astype(BF16)
    dg[:, :512] = g1
    dg[:, 512:] = g2
    da = dot_nt(g1, w[:, :512]) + dot_nt(g2, w[:, 512:])
    n3, inv3 = norm(x2[0])
    sums[0:1] = column_sum(da * n3)
    sums[1:8] = jnp.zeros((7, D), F32)
    out = dx3[...] + norm_back(da, n3, inv3, gain_c)
    dx2[...] = out
    e2[...] = out.astype(BF16)


def attend_back_kernel(
    idx, x1, gain, cos, sin, dx2a, dx2b, q, k, v, pr, jm, jo, om, oo,
    dj, dx1, e1, sums, wj, wo, dmix, dq, dkey, sem,
):
    micro = pl.program_id(0)

    @pl.when(micro == 0)
    def _():
        fetch(idx[0], ((jm, jo), (om, oo)), (wj, wo), sem)
        dx1[0] = dx2a[...]

    @pl.when(micro == 1)
    def _():
        dx1[0] = dx2b[...]

    grad2 = dx1[0]
    dmix[...] = dot_nt(grad2.astype(BF16), wo[...]).astype(BF16)
    masks = head_masks()

    def pair(p, carry):
        c = pl.ds(pl.multiple_of(p * 128, 128), 128)
        qp, kp, vp, gp = q[0, :, c], k[0, :, c], v[0, :, c], dmix[:, c]
        parts = [None, None, None]
        for e in range(2):
            prob = pr[0, 2 * p + e]
            grad = gp * masks[e]
            dp = dot_nt(grad, vp)
            wide = prob.astype(F32)
            prod = wide * dp
            ds = (prod - wide * jnp.sum(prod, axis=-1, keepdims=True)).astype(BF16)
            new = (dot(ds, kp * masks[e]), dot_tn(ds, qp * masks[e]), dot_tn(prob, grad))
            parts = [b if a is None else a + b for a, b in zip(parts, new)]
        dq[:, c] = parts[0]
        dkey[:, c] = parts[1]
        dj[0, :, pl.ds(pl.multiple_of(1024 + p * 128, 128), 128)] = parts[2].astype(BF16)
        return carry

    lax.fori_loop(0, HEADS // 2, pair, 0)
    cosine, sine = cos[0], -sin[0]
    dj[0, :, :512] = turn(dq[...] * HDIM ** (-0.5), cosine, sine).astype(BF16)
    dj[0, :, 512:1024] = turn(dkey[...], cosine, sine).astype(BF16)
    da = dot_nt(dj[0], wj[...])
    n2, inv2 = norm(x1[0])
    sums[0, 0:1] = column_sum(da * n2)
    sums[0, 1:8] = jnp.zeros((7, D), F32)
    out = grad2 + norm_back(da, n2, inv2, gain[...])
    dx1[0] = out
    e1[0] = (0.5 * out).astype(BF16)


def feed_back_kernel(idx, x, gain, dx1, e1, g1, um, uo, dm, do, fg, dz, sums, u, d, sem):
    @pl.when(pl.program_id(0) == 0)
    def _():
        fetch(idx[0], ((um, uo), (dm, do)), (u, d), sem)
        sums[...] = jnp.zeros(sums.shape, F32)

    e = e1[...]
    acc = None
    for j in range(4):
        c = slice(j * 512, (j + 1) * 512)
        g = (dot_nt(e, d[c, :]) * g1[:, c].astype(F32)).astype(BF16)
        dz[:, c] = g
        part = dot_nt(g, u[:, c])
        acc = part if acc is None else acc + part
    n1, inv1 = norm(x[...].astype(F32))
    sums[0:1] += column_sum(acc * n1)
    fg[...] = (dx1[...] + norm_back(acc, n1, inv1, gain[...])).astype(BF16)


def weight_kernel(plan, core, *refs):
    ins, (send, keep) = refs[:-2], refs[-2:]
    step = pl.program_id(0)

    def fill(out):
        at = 0
        for i, blocks in enumerate(plan):
            l0, r0, l1, r1 = ins[4 * i : 4 * i + 4]
            rows = l0.shape[1]
            for j in range(blocks):
                c = slice(j * 512, (j + 1) * 512)
                out[0, at : at + rows] = (
                    dot_tn(l0[...], r0[:, c]) + dot_tn(l1[...], r1[:, c])
                ).astype(BF16)
                at += rows

    @pl.when(step < 2)
    def _():
        fill(send)

    @pl.when(step >= 2)
    def _():
        fill(keep)


def full(shape):
    zeros = (0,) * len(shape)
    return pl.BlockSpec(shape, lambda *_: zeros)


def out(shape, dtype):
    return jax.ShapeDtypeStruct(shape, dtype)


def cost(flops, nbytes):
    return pl.CostEstimate(flops=int(flops), bytes_accessed=int(nbytes), transcendentals=0)


def micro_spec(shape, micro):
    rest = (0,) * len(shape)
    return pl.BlockSpec((1,) + shape, lambda *_: (micro,) + rest)


def weight_call(name, products, core):
    plan, specs, arrays, rows, flops = [], [], [], 0, 0

    def quarter(step, core_ref):
        x = step % 2
        mine = core_ref[0]
        return x * 2 + jnp.where(step < 2, 1 - mine, mine)

    for l0, r0, l1, r1 in products:
        slots, m = l0.shape
        n = r0.shape[1]
        plan.append(n // 512)
        rows += (n // 512) * (m // 4)
        flops += 4 * slots * m * n
        for left, right in ((l0, r0), (l1, r1)):
            specs.append(pl.BlockSpec((slots, m // 4), lambda s, ref: (0, quarter(s, ref))))
            specs.append(pl.BlockSpec((slots, n), lambda s, ref: (0, 0)))
            arrays += [left, right]
    nbytes = sum(a.size * 2 for a in arrays) + rows * 512 * 8
    return pl.pallas_call(
        functools.partial(weight_kernel, tuple(plan)),
        name=name,
        grid_spec=pltpu.PrefetchScalarGridSpec(
            num_scalar_prefetch=1,
            grid=(4,),
            in_specs=specs,
            out_specs=[
                pl.BlockSpec((1, rows, D), lambda s, ref: (jnp.minimum(s, 1), 0, 0)),
                pl.BlockSpec((1, rows, D), lambda s, ref: (jnp.maximum(s - 2, 0), 0, 0)),
            ],
        ),
        out_shape=[out((2, rows, D), BF16)] * 2,
        cost_estimate=cost(flops, nbytes),
    )(core, *arrays)


def unpack(reduced, shapes):
    found, at = [], 0
    for m, n in shapes:
        rows = (n // 512) * (m // 4)
        part = reduced[:, at : at + rows].astype(F32).reshape(2, n // 512, m // 4, 512)
        found.append(part.transpose(0, 2, 1, 3).reshape(m // 2, n))
        at += rows
    return found


def layout(lengths, mask, slots):
    ends = jnp.cumsum(lengths, axis=1)
    starts = ends - lengths
    slot = jnp.arange(slots, dtype=jnp.int32)
    reached = slot[None, :, None] >= ends[:, None, :]
    segment = jnp.sum(reached.astype(jnp.int32), axis=2)
    member = segment[:, :, None] == jnp.arange(lengths.shape[1], dtype=jnp.int32)
    begin = jnp.sum(jnp.where(member, starts[:, None, :], 0), axis=2)
    end = jnp.sum(jnp.where(member, ends[:, None, :], 0), axis=2)
    return segment, slot[None] - begin, end - 1 - slot[None]


def body(
    sizes, frames, item_lengths, frame_mask, first_norm, first_up, first_down, attend_norm,
    attend_joint, attend_out, conv_norm, conv_in, conv_kern, batch_gain, batch_bias, conv_out,
    second_norm, second_up, second_down, final_norm, output_grad,
):
    slots = frames.shape[1]
    x_at = lax.axis_index("fsdp").astype(jnp.int32).reshape(1)
    core = (lax.axis_index("dp") & 1).astype(jnp.int32).reshape(1)
    first_x = lax.axis_index("fsdp") == 0

    def other(shard):
        return swap(shard, "fsdp", 1, 2)

    norms = jnp.stack(
        [first_norm, attend_norm, conv_norm, batch_gain, batch_bias, second_norm, final_norm]
    )
    norms_o = other(norms)
    gains = jnp.concatenate(
        [jnp.where(first_x, norms, norms_o), jnp.where(first_x, norms_o, norms)], axis=1
    ).astype(F32)
    kern_o = other(conv_kern)
    kern = jnp.concatenate(
        [jnp.where(first_x, conv_kern, kern_o), jnp.where(first_x, kern_o, conv_kern)], axis=0
    ).astype(F32)
    up1, down1, joint, aout, cin, cout_w, up2, down2 = (
        (w, other(w))
        for w in (
            first_up, first_down, attend_joint, attend_out, conv_in, conv_out, second_up, second_down
        )
    )
    g_first, g_attend, g_conv, g_bn, b_bn, g_second, g_final = (
        gains[i : i + 1] for i in range(7)
    )
    segment, position, left = layout(item_lengths[:, 0], frame_mask, slots)
    half = HDIM // 2
    freq = jnp.exp(jnp.arange(half, dtype=F32) * (-2.0 * math.log(10000.0) / HDIM))
    angle = position.astype(F32)[:, :, None] * freq
    cosine, sine = jnp.cos(angle), jnp.sin(angle)
    cos_t = jnp.concatenate([cosine] * 4, axis=-1)
    sin_t = jnp.concatenate([-sine, sine, -sine, sine], axis=-1)
    valid = frame_mask.astype(F32)

    def wide(values):
        return jnp.broadcast_to(values.astype(F32)[:, :, None], (MB, slots, 128))

    segb, before, after, validb = wide(segment), wide(position), wide(left), wide(valid)
    rows = jnp.stack([segment.astype(F32), valid], axis=1)

    tall = MB * slots
    tm = 256
    x_flat = frames.reshape(tall, D)

    def row_spec(width):
        return pl.BlockSpec((tm, width), lambda i: (i, 0))

    x1, a1, h1, g1 = pl.pallas_call(
        feed_kernel,
        name="feed",
        grid=(tall // tm,),
        in_specs=[SMEM, row_spec(D), full((1, D)), ANY, ANY, ANY, ANY],
        out_specs=[row_spec(D), row_spec(D), row_spec(FF), row_spec(FF)],
        out_shape=[out((tall, D), F32), out((tall, D), BF16)] + [out((tall, FF), BF16)] * 2,
        scratch_shapes=weight_scratch((D, FF), (FF, D)),
        cost_estimate=cost(4 * tall * D * FF, 2e7),
    )(x_at, x_flat, g_first, *up1, *down1)

    def cut(array):
        return array.reshape(MB, slots, array.shape[-1])

    def by_micro(*shape):
        rest = (0,) * len(shape)
        return pl.BlockSpec((1,) + shape, lambda i: (i,) + rest)

    x1 = cut(x1)
    x2, a2, qh, kh, vh, probs, mixed = pl.pallas_call(
        attend_kernel,
        name="attend",
        grid=(MB,),
        in_specs=[
            SMEM, by_micro(slots, D), full((1, D)), by_micro(slots, 128), by_micro(slots, 128),
            by_micro(slots, 128), by_micro(2, slots), ANY, ANY, ANY, ANY,
        ],
        out_specs=[by_micro(slots, D)] * 5 + [by_micro(HEADS, slots, slots), by_micro(slots, D)],
        out_shape=[out((MB, slots, D), F32)] + [out((MB, slots, D), BF16)] * 4
        + [out((MB, HEADS, slots, slots), BF16), out((MB, slots, D), BF16)],
        scratch_shapes=[
            pltpu.VMEM((D, 3 * D), BF16), pltpu.VMEM((D, D), BF16), pltpu.VMEM((slots, slots), F32),
            pltpu.SemaphoreType.DMA((4,)),
        ],
        cost_estimate=cost(MB * slots * (8 * D * D + 8 * slots * D), 3e7),
    )(x_at, x1, g_attend, cos_t, sin_t, segb, rows, *joint, *aout)

    pad_rows = slots + 40

    def forward_conv(m):
        return pl.pallas_call(
            conv_kernel,
            name=f"conv_{m}",
            in_specs=[
                SMEM, micro_spec((slots, D), m), full((1, D)), full((KER, D)),
                *[micro_spec((slots, 128), m)] * 3, ANY, ANY,
            ],
            out_specs=[full((slots, D))] * 5 + [full((8, D))],
            grid=(1,),
            out_shape=[
                out((slots, D), BF16), out((slots, D), F32), out((slots, D), BF16),
                out((slots, D), BF16), out((slots, D), F32), out((8, D), F32),
            ],
            scratch_shapes=[
                pltpu.VMEM((D, 2 * D), BF16), pltpu.VMEM((pad_rows, D), F32),
                pltpu.VMEM((8, pad_rows - 8, D), F32), pltpu.SemaphoreType.DMA((2,)),
            ],
            cost_estimate=cost(4 * slots * D * D + 60 * KER * slots * D, 1e7),
        )(x_at, x2, g_conv, kern, validb, before, after, *cin)

    convs = [forward_conv(m) for m in range(MB)]
    totals = [sum_all(c[5], sizes) for c in convs]
    mid_gains = jnp.concatenate([g_bn, b_bn, g_second, g_final], axis=0)

    def middle(m):
        def at_micro(width):
            return pl.BlockSpec((1, tm, width), lambda i: (m, i, 0))

        return pl.pallas_call(
            middle_kernel,
            name=f"middle_{m}",
            grid=(slots // tm,),
            in_specs=[
                SMEM, full((8, D)), full((4, D)), row_spec(D), at_micro(D), at_micro(D),
                ANY, ANY, ANY, ANY, ANY, ANY,
            ],
            out_specs=[row_spec(D)] * 4 + [row_spec(FF)] * 2 + [row_spec(D)] * 3 + [full((8, D))],
            out_shape=[out((slots, D), BF16)] * 4 + [out((slots, FF), BF16)] * 2
            + [out((slots, D), BF16)] + [out((slots, D), F32)] * 2 + [out((8, D), F32)],
            scratch_shapes=[
                pltpu.VMEM((D, D), BF16), pltpu.VMEM((D, FF), BF16), pltpu.VMEM((FF, D), BF16),
                pltpu.VMEM((tm, FF), BF16), pltpu.SemaphoreType.DMA((6,)),
            ],
            cost_estimate=cost(slots * (8 * D * FF + 4 * D * D), 2e7),
        )(x_at, totals[m], mid_gains, convs[m][4], x2, output_grad, *cout_w, *up2, *down2)

    mids = [middle(m) for m in range(MB)]
    backs = [sum_all(mid[9], sizes) for mid in mids]
    enc = jnp.stack([mid[0] for mid in mids])

    def product(lefts, rights):
        return (lefts[0], rights[0], lefts[1], rights[1])

    a4, e3, a5, h2, dz2, e4 = ([mid[i] for mid in mids] for i in range(1, 7))
    send, keep = weight_call(
        "weights_second", [product(h2, e4), product(a5, dz2), product(a4, e3)], core
    )
    sum_second = reduce_rows(send, keep, sizes)
    back_gains = jnp.concatenate([g_bn, g_conv], axis=0)

    def back_conv(m):
        a3, glu, p1, p2, conv, _ = convs[m]
        return pl.pallas_call(
            conv_back_kernel,
            name=f"conv_back_{m}",
            grid=(1,),
            in_specs=[
                SMEM, full((8, D)), full((8, D)), full((2, D)), full((KER, D)),
                *[full((slots, D))] * 5, micro_spec((slots, D), m), full((slots, D)),
                *[micro_spec((slots, 128), m)] * 3, ANY, ANY,
            ],
            out_specs=[
                full((slots, 2 * D)), full((slots, D)), full((slots, D)), full((KER, D)), full((8, D)),
            ],
            out_shape=[
                out((slots, 2 * D), BF16), out((slots, D), F32), out((slots, D), BF16),
                out((KER, D), F32), out((8, D), F32),
            ],
            scratch_shapes=[
                pltpu.VMEM((D, 2 * D), BF16), pltpu.VMEM((pad_rows, D), F32),
                pltpu.VMEM((8, pad_rows - 8, D), F32), pltpu.VMEM((slots, D), F32),
                pltpu.VMEM((KER, 8, D), F32), pltpu.SemaphoreType.DMA((2,)),
            ],
            cost_estimate=cost(4 * slots * D * D + 120 * KER * slots * D, 1.5e7),
        )(x_at, totals[m], backs[m], back_gains, kern, conv, mids[m][7], glu, p1, p2, x2, mids[m][8],
          validb, before, after, *cin)

    conv_backs = [back_conv(m) for m in range(MB)]
    dj, dx1, e1, sums_attend = pl.pallas_call(
        attend_back_kernel,
        name="attend_back",
        grid=(MB,),
        in_specs=[
            SMEM, by_micro(slots, D), full((1, D)), by_micro(slots, 128), by_micro(slots, 128),
            full((slots, D)), full((slots, D)), *[by_micro(slots, D)] * 3,
            by_micro(HEADS, slots, slots), ANY, ANY, ANY, ANY,
        ],
        out_specs=[by_micro(slots, 3 * D), by_micro(slots, D), by_micro(slots, D), by_micro(8, D)],
        out_shape=[
            out((MB, slots, 3 * D), BF16), out((MB, slots, D), F32), out((MB, slots, D), BF16),
            out((MB, 8, D), F32),
        ],
        scratch_shapes=[
            pltpu.VMEM((D, 3 * D), BF16), pltpu.VMEM((D, D), BF16), pltpu.VMEM((slots, D), BF16),
            pltpu.VMEM((slots, D), F32), pltpu.VMEM((slots, D), F32), pltpu.SemaphoreType.DMA((4,)),
        ],
        cost_estimate=cost(MB * slots * (8 * D * D + 16 * slots * D), 3e7),
    )(x_at, x1, g_attend, cos_t, sin_t, conv_backs[0][1], conv_backs[1][1], qh, kh, vh, probs,
      *joint, *aout)
    send, keep = weight_call(
        "weights_attend",
        [
            product([c[0] for c in convs], [c[0] for c in conv_backs]),
            product(mixed, [c[2] for c in conv_backs]),
            product(a2, dj),
        ],
        core,
    )
    sum_attend = reduce_rows(send, keep, sizes)
    h1, a1 = cut(h1), cut(a1)
    send, keep = weight_call("weights_down", [product(h1, e1)], core)
    sum_down = reduce_rows(send, keep, sizes)
    fgrad, dz1, sums_first = pl.pallas_call(
        feed_back_kernel,
        name="feed_back",
        grid=(tall // tm,),
        in_specs=[
            SMEM, row_spec(D), full((1, D)), row_spec(D), row_spec(D), row_spec(FF), ANY, ANY, ANY, ANY,
        ],
        out_specs=[row_spec(D), row_spec(FF), full((8, D))],
        out_shape=[out((tall, D), BF16), out((tall, FF), BF16), out((8, D), F32)],
        scratch_shapes=weight_scratch((D, FF), (FF, D)),
        cost_estimate=cost(4 * tall * D * FF, 2e7),
    )(x_at, x_flat, g_first, dx1.reshape(tall, D), e1.reshape(tall, D), g1, *up1, *down1)
    dz1 = cut(dz1)
    send, keep = weight_call("weights_up", [product(a1, dz1)], core)
    sum_up = reduce_rows(send, keep, sizes)

    mid_sums = mids[0][9] + mids[1][9]
    small = jnp.concatenate(
        [
            conv_backs[0][3] + conv_backs[1][3],
            sums_first[0:1],
            sums_attend[0, 0:1] + sums_attend[1, 0:1],
            conv_backs[0][4][0:1] + conv_backs[1][4][0:1],
            mid_sums[1:2],
            mid_sums[0:1],
            mid_sums[2:4],
            jnp.zeros((1, D), F32),
        ],
        axis=0,
    )
    small = sum_all(small, sizes)
    kern_grad = lax.dynamic_slice_in_dim(small, x_at[0] * (KER // 2), KER // 2, axis=0)
    vectors = lax.dynamic_slice_in_dim(small[KER:], x_at[0] * (D // 2), D // 2, axis=1)

    down2_g, up2_g, cout_g = unpack(sum_second, [(FF, D), (D, FF), (D, D)])
    cin_g, aout_g, joint_g = unpack(sum_attend, [(D, 2 * D), (D, D), (D, 3 * D)])
    (down1_g,) = unpack(sum_down, [(FF, D)])
    (up1_g,) = unpack(sum_up, [(D, FF)])
    return (
        enc, fgrad.reshape(MB, slots, D), vectors[0], up1_g, down1_g, vectors[1], joint_g, aout_g,
        vectors[2], cin_g, kern_grad, vectors[3], vectors[4], cout_g, vectors[5], up2_g, down2_g,
        vectors[6],
    )


def solution(mesh):
    split = P(None, ("dp", "fsdp"), None)
    row, mat = P("fsdp"), P("fsdp", None)
    weights = (row, mat, mat, row, mat, mat, row, mat, mat, row, row, mat, row, mat, mat, row)
    return jax.shard_map(
        functools.partial(body, dict(mesh.shape)),
        mesh=mesh,
        in_specs=(split, split, P(None, ("dp", "fsdp"))) + weights + (split,),
        out_specs=(split, split) + weights,
        check_vma=False,
    )
```

```python
import functools
import math

import jax
import jax.numpy as jnp
from jax import lax
from jax.experimental import pallas as pl
from jax.experimental.pallas import tpu as pltpu
from jax.sharding import PartitionSpec as P

HEADS = 8
KER = 32
HDIM = 64
MB = 2
D = 512
FF = 2048
EPS = 1e-05
PAD = 16
CHUNK = 32
F32 = jnp.float32
BF16 = jnp.bfloat16
ANY = pl.BlockSpec(memory_space=pl.ANY)
SMEM = pl.BlockSpec(memory_space=pltpu.SMEM)
VMEM = pl.BlockSpec(memory_space=pltpu.VMEM)


def swap(value, axis, bit, size):
    return lax.ppermute(value, axis, [(i, i ^ bit) for i in range(size)])


def bits_of(size):
    return [1 << i for i in range(size.bit_length() - 1)]


class Line:
    def __init__(self):
        self.last = ()

    def after(self, value):
        return lax.optimization_barrier((value,) + self.last)[0] if self.last else value

    def did(self, *values):
        self.last = values


def add_split(keep, got, index):
    parts = []
    for at in (index, 1 - index):
        left = lax.dynamic_index_in_dim(keep, at, 0, keepdims=False)
        right = lax.dynamic_index_in_dim(got, at, 0, keepdims=False)
        parts.append((left.astype(F32) + right.astype(F32)).astype(BF16))
    return parts


def unpack_kernel(shapes, index, keep, got, *outs):
    at = 0
    for (m, n), target in zip(shapes, outs):
        quarter = m // 4
        for source, core in ((keep, index[0]), (got, 1 - index[0])):
            rows = pl.ds(pl.multiple_of(core * quarter, quarter), quarter)
            for j in range(n // 512):
                first = at + j * quarter
                target[rows, j * 512 : (j + 1) * 512] = source[first : first + quarter].astype(F32)
        at += (n // 512) * quarter


class Chain:
    def __init__(self, line, sizes, shapes, send, keep, halved):
        self.line, self.sizes, self.shapes, self.keep = line, sizes, shapes, keep
        bits = bits_of(sizes["dp"])[1:]
        halved = bits[:halved]
        whole = bits[len(halved) :]
        self.plan = [("split", "x")] + [("split", bit) for bit in halved] + [("add", bit) for bit in whole]
        self.plan += [("last", None)] + [("join", bit) for bit in halved[::-1]] + [("unpack", 1)]
        self.order = ["x"] + halved + whole + halved[::-1] + [1]
        self.got = swap(send, "dp", 1, sizes["dp"])
        self.result = None

    def where(self, bit):
        if bit == "x":
            return lax.axis_index("fsdp").astype(jnp.int32)
        return ((lax.axis_index("dp") & bit) > 0).astype(jnp.int32)

    def send(self, value):
        bit = self.order.pop(0)
        if bit == "x":
            self.got = swap(value, "fsdp", 1, 2)
        else:
            self.got = swap(value, "dp", bit, self.sizes["dp"])

    def step(self):
        kind, bit = self.plan.pop(0)
        got = self.line.after(self.got)
        keep = self.keep
        if kind == "split":
            rows = keep.size // (2 * D)
            self.keep, send = add_split(keep.reshape(2, rows, D), got.reshape(2, rows, D), self.where(bit))
            self.line.did(send, self.keep)
            self.send(send)
        elif kind in ("add", "last"):
            self.keep = (keep.astype(F32) + got.astype(F32)).astype(BF16)
            self.line.did(self.keep)
            self.send(self.keep)
        elif kind == "join":
            low = self.where(bit) == 0
            self.keep = jnp.concatenate([jnp.where(low, keep, got), jnp.where(low, got, keep)], axis=0)
            self.line.did(self.keep)
            self.send(self.keep)
        else:
            outs = [out((m // 2, n), F32) for m, n in self.shapes]
            self.result = pl.pallas_call(
                functools.partial(unpack_kernel, self.shapes),
                name="unpack",
                in_specs=[SMEM, VMEM, VMEM],
                out_specs=[VMEM] * len(outs),
                out_shape=outs,
                cost_estimate=cost(0, 12 * keep.size),
            )(self.where(1).reshape(1), keep, got)
            self.line.did(self.result[-1])


class Background(Chain):
    def __init__(self, line, sizes, shapes, send, keep):
        super().__init__(line, sizes, shapes, send, keep, 0)
        self.plan = [("split", "x"), ("total", None), ("unpack", 1)]

    def step(self):
        if self.plan[0][0] != "total":
            return super().step()
        self.plan.pop(0)
        got = self.line.after(self.got)
        self.keep = (self.keep.astype(F32) + got.astype(F32)).astype(BF16)
        self.line.did(self.keep)

    def pass_on(self):
        self.keep = self.line.after(self.keep)
        self.got = swap(self.keep, "dp", 1, self.sizes["dp"])


def reduce_behind(chains, size):
    groups = [[i for i in range(size) if i % 2 == c] for c in range(2)]
    totals = lax.psum(tuple(c.keep for c in chains), "dp", axis_index_groups=groups)
    for chain, total in zip(chains, totals):
        chain.keep = total


class Sum:
    def __init__(self, line, sizes, value):
        self.line, self.sizes, self.value = line, sizes, value
        self.plan = bits_of(sizes["dp"]) + ["x"]
        self.start()

    def start(self):
        bit = self.plan.pop(0)
        if bit == "x":
            self.got = swap(self.value, "fsdp", 1, 2)
        else:
            self.got = swap(self.value, "dp", bit, self.sizes["dp"])

    def step(self):
        self.value = self.value + self.line.after(self.got)
        self.line.did(self.value)
        if self.plan:
            self.start()
            return True
        return False


def dot(left, right):
    return lax.dot_general(left, right, (((1,), (0,)), ((), ())), preferred_element_type=F32)


def dot_nt(left, right):
    return lax.dot_general(left, right, (((1,), (1,)), ((), ())), preferred_element_type=F32)


def dot_tn(left, right):
    return lax.dot_general(left, right, (((0,), (0,)), ((), ())), preferred_element_type=F32)


def sigmoid(values):
    return 0.5 * jnp.tanh(0.5 * values) + 0.5


def norm(values):
    centered = values - jnp.mean(values, axis=-1, keepdims=True)
    inverse = lax.rsqrt(jnp.mean(centered * centered, axis=-1, keepdims=True) + EPS)
    return centered * inverse, inverse


def norm_back(grad, rows, inverse, gain):
    scaled = grad * gain
    return inverse * (
        scaled
        - jnp.mean(scaled, axis=-1, keepdims=True)
        - rows * jnp.mean(scaled * rows, axis=-1, keepdims=True)
    )


def column_sum(values):
    return jnp.sum(values, axis=0, keepdims=True)


def fetch(where, sources, targets, sem):
    copies = []
    for i, (mine, near, far) in enumerate(sources):
        rows = mine.shape[0]
        piece = rows // 2
        start = (1 - where[0]) * rows
        places = (where[0] * rows, start + where[1] * piece, start + (1 - where[1]) * piece)
        for j, source in enumerate((mine, near, far)):
            at = pl.multiple_of(places[j], piece)
            copies.append(
                pltpu.make_async_copy(
                    source, targets[i].at[pl.ds(at, source.shape[0])], sem.at[3 * i + j]
                )
            )
    for copy in copies:
        copy.start()
    for copy in copies:
        copy.wait()


def weight_scratch(*shapes):
    return [pltpu.VMEM(shape, BF16) for shape in shapes] + [
        pltpu.SemaphoreType.DMA((3 * len(shapes),))
    ]


def tile4(values):
    return jnp.concatenate([values] * 4, axis=1)


def turn(values, cosine, sine):
    lane = lax.broadcasted_iota(jnp.int32, (values.shape[0], 128), 1)
    first = (lane & 63) < 32
    parts = []
    for c in range(4):
        u = values[:, c * 128 : (c + 1) * 128]
        swapped = jnp.where(first, pltpu.roll(u, 96, 1), pltpu.roll(u, 32, 1))
        parts.append(u * cosine + swapped * sine)
    return jnp.concatenate(parts, axis=1)


def head_masks():
    lane = lax.broadcasted_iota(jnp.int32, (1, 128), 1)
    return [((lane >> 6) == e).astype(F32).astype(BF16) for e in range(2)]


def feed_kernel(idx, x, gain, um, un, uf, dm, dn, df, x1, a1, h1, g1, u, d, sem):
    @pl.when(pl.program_id(0) == 0)
    def _():
        fetch(idx, ((um, un, uf), (dm, dn, df)), (u, d), sem)

    v = x[...].astype(F32)
    a = (norm(v)[0] * gain[...]).astype(BF16)
    a1[...] = a
    acc = None
    for j in range(4):
        c = slice(j * 512, (j + 1) * 512)
        z = dot(a, u[:, c])
        s = sigmoid(z)
        h = z * s
        g1[:, c] = (s + h * (1.0 - s)).astype(BF16)
        h = h.astype(BF16)
        h1[:, c] = h
        part = dot(h, d[c, :])
        acc = part if acc is None else acc + part
    x1[...] = v + 0.5 * acc


def attend_kernel(
    idx, x1, gain, cos, sin, segb, rows, jm, jn, jf, om, on, of,
    x2, a2, qo, ko, vo, pr, mixed, wj, wo, bias, sem,
):
    @pl.when(pl.program_id(0) == 0)
    def _():
        fetch(idx, ((jm, jn, jf), (om, on, of)), (wj, wo), sem)

    v = x1[0]
    a = (norm(v)[0] * gain[...]).astype(BF16)
    a2[0] = a
    cosine, sine = cos[0], sin[0]
    qo[0] = (turn(dot(a, wj[:, :512]), cosine, sine) * HDIM ** (-0.5)).astype(BF16)
    ko[0] = turn(dot(a, wj[:, 512:1024]), cosine, sine).astype(BF16)
    vo[0] = dot(a, wj[:, 1024:]).astype(BF16)
    size = bias.shape[0]
    row = lax.broadcasted_iota(jnp.int32, (size, size), 0)
    col = lax.broadcasted_iota(jnp.int32, (size, size), 1)
    allowed = (tile4(segb[0]) == rows[0, 0:1, :]) & ((rows[0, 1:2, :] > 0) | (row == col))
    bias[...] = jnp.where(allowed, 0.0, -1000000000.0)
    masks = head_masks()

    def pair(p, carry):
        c = pl.ds(pl.multiple_of(p * 128, 128), 128)
        q, k, val = qo[0, :, c], ko[0, :, c], vo[0, :, c]
        total = None
        for e in range(2):
            s = dot_nt(q * masks[e], k) + bias[...]
            ex = jnp.exp(s - jnp.max(s, axis=-1, keepdims=True))
            prob = (ex * (1.0 / jnp.sum(ex, axis=-1, keepdims=True))).astype(BF16)
            pr[0, 2 * p + e] = prob
            part = dot(prob, val * masks[e])
            total = part if total is None else total + part
        mixed[0, :, c] = total.astype(BF16)
        return carry

    lax.fori_loop(0, HEADS // 2, pair, 0)
    x2[0] = v + dot(mixed[0], wo[...])


def conv_taps(padded, shifts):
    rows = shifts.shape[1]
    for b in range(8):
        shifts[b] = padded[b : b + rows, :]


def conv_kernel(
    idx, inside, x2, gain, kern, validb, before, after, wm, wn, wf,
    a3, glu, p1, p2, cout, stats, w, padded, shifts, sem,
):
    micro = pl.program_id(0)
    size = x2.shape[1]

    @pl.when(micro == 0)
    def _():
        fetch(idx, ((wm, wn, wf),), (w,), sem)
        padded[0:PAD] = jnp.zeros((PAD, D), F32)
        padded[PAD + size :] = jnp.zeros((padded.shape[0] - PAD - size, D), F32)

    a = (norm(x2[0])[0] * gain[...]).astype(BF16)
    a3[0] = a
    valid = tile4(validb[0])
    g1 = dot(a, w[:, :512])
    s = sigmoid(dot(a, w[:, 512:])) * valid
    g = g1 * s
    glu[0] = g
    p1[0] = s.astype(BF16)
    p2[0] = (g * (1.0 - s)).astype(BF16)
    padded[PAD : PAD + size] = g
    conv_taps(padded, shifts)

    def step(i, carry):
        r0 = pl.multiple_of(i * CHUNK, CHUNK)

        def run(masked):
            if masked:
                low, high = before[0, pl.ds(r0, CHUNK), :], after[0, pl.ds(r0, CHUNK), :]
            acc = [jnp.zeros((CHUNK, 128), F32) for _ in range(4)]
            for o in range(KER):
                shift_by = o - (KER - 1) // 2
                a8, b = divmod(shift_by + PAD, 8)
                if masked and shift_by < 0:
                    keep = low >= float(-shift_by)
                elif masked and shift_by > 0:
                    keep = high >= float(shift_by)
                for c in range(4):
                    cs = slice(c * 128, (c + 1) * 128)
                    value = shifts[b, pl.ds(r0 + 8 * a8, CHUNK), cs]
                    if masked and shift_by != 0:
                        value = jnp.where(keep, value, 0.0)
                    acc[c] = acc[c] + kern[o : o + 1, cs] * value
            for c in range(4):
                cout[0, pl.ds(r0, CHUNK), c * 128 : (c + 1) * 128] = acc[c]

        flag = inside[micro, i]
        pl.when(flag > 0)(functools.partial(run, False))
        pl.when(flag == 0)(functools.partial(run, True))
        return carry

    lax.fori_loop(0, size // CHUNK, step, 0)
    result = cout[0]
    weighted = result * valid
    stats[0, 0:1] = column_sum(weighted)
    stats[0, 1:2] = column_sum(weighted * result)
    stats[0, 2:3] = column_sum(valid)
    stats[0, 3:4] = jnp.zeros((1, D), F32)


def middle_kernel(
    idx, total, gains, conv, x2, og, cm, cn, cf, um, un, uf, dm, dn, df,
    enc, a4, e3, a5, h2, dz, e4, db, dx3, sums, wc, u, d, deriv, sem,
):
    @pl.when((pl.program_id(0) == 0) & (pl.program_id(1) == 0))
    def _():
        fetch(idx, ((cm, cn, cf), (um, un, uf), (dm, dn, df)), (wc, u, d), sem)

    @pl.when(pl.program_id(1) == 0)
    def _():
        sums[...] = jnp.zeros(sums.shape, F32)

    gain_b, bias_b, gain_2, gain_f = (gains[i : i + 1] for i in range(4))
    count = total[0, 2:3]
    mean = total[0, 0:1] / count
    inverse = lax.rsqrt(total[0, 1:2] / count - mean * mean + EPS)
    unit = (conv[...] - mean) * inverse
    act = unit * gain_b + bias_b
    s_act = sigmoid(act)
    a = (act * s_act).astype(BF16)
    a4[...] = a
    v3 = x2[...] + dot(a, wc[...])
    n5, inv5 = norm(v3)
    a = (n5 * gain_2).astype(BF16)
    a5[...] = a
    acc = None
    for j in range(4):
        c = slice(j * 512, (j + 1) * 512)
        z = dot(a, u[:, c])
        s = sigmoid(z)
        h = z * s
        deriv[:, c] = (s + h * (1.0 - s)).astype(BF16)
        h = h.astype(BF16)
        h2[:, c] = h
        part = dot(h, d[c, :])
        acc = part if acc is None else acc + part
    n6, inv6 = norm(v3 + 0.5 * acc)
    enc[...] = (n6 * gain_f).astype(BF16)
    dy = og[...].astype(F32)
    sums[0, 3:4] += column_sum(dy * n6)
    grad4 = norm_back(dy, n6, inv6, gain_f)
    e = (0.5 * grad4).astype(BF16)
    e4[...] = e
    acc = None
    for j in range(4):
        c = slice(j * 512, (j + 1) * 512)
        g = (dot_nt(e, d[c, :]) * deriv[:, c].astype(F32)).astype(BF16)
        dz[:, c] = g
        part = dot_nt(g, u[:, c])
        acc = part if acc is None else acc + part
    sums[0, 2:3] += column_sum(acc * n5)
    grad3 = grad4 + norm_back(acc, n5, inv5, gain_2)
    dx3[...] = grad3
    e = grad3.astype(BF16)
    e3[...] = e
    dact = dot_nt(e, wc[...]) * (s_act * (1.0 + act * (1.0 - s_act)))
    db[...] = dact
    sums[0, 0:1] += column_sum(dact)
    sums[0, 1:2] += column_sum(dact * unit)


def conv_back_kernel(
    idx, inside, total, back, gains, kern, conv, db, glu, p1, p2, x2, dx3, validb, before, after, wm, wn, wf,
    dg, dx2, e2, dk, sums, w, padded, shifts, dglu, dkacc, sem,
):
    micro = pl.program_id(0)
    size = x2.shape[1]

    @pl.when(micro == 0)
    def _():
        fetch(idx, ((wm, wn, wf),), (w,), sem)
        padded[0:PAD] = jnp.zeros((PAD, D), F32)
        padded[PAD + size :] = jnp.zeros((padded.shape[0] - PAD - size, D), F32)
        dkacc[...] = jnp.zeros(dkacc.shape, F32)

    gain_b, gain_c = gains[0:1], gains[1:2]
    count = total[0, 2:3]
    mean = total[0, 0:1] / count
    inverse = lax.rsqrt(total[0, 1:2] / count - mean * mean + EPS)
    share = inverse / count
    at_one, at_unit = share * (gain_b * back[0, 0:1]), share * (gain_b * back[0, 1:2])
    unit = (conv[0] - mean) * inverse
    padded[PAD : PAD + size] = db[0] * (inverse * gain_b) - tile4(validb[0]) * (at_one + unit * at_unit)
    conv_taps(padded, shifts)

    def step(i, carry):
        r0 = pl.multiple_of(i * CHUNK, CHUNK)

        def run(masked):
            if masked:
                low, high = before[0, pl.ds(r0, CHUNK), :], after[0, pl.ds(r0, CHUNK), :]
            for c in range(4):
                cs = slice(c * 128, (c + 1) * 128)
                own = glu[0, pl.ds(r0, CHUNK), cs]
                acc = jnp.zeros((CHUNK, 128), F32)
                for o in range(KER):
                    shift_by = (KER - 1) // 2 - o
                    a8, b = divmod(shift_by + PAD, 8)
                    value = shifts[b, pl.ds(r0 + 8 * a8, CHUNK), cs]
                    if masked and shift_by < 0:
                        value = jnp.where(low >= float(-shift_by), value, 0.0)
                    elif masked and shift_by > 0:
                        value = jnp.where(high >= float(shift_by), value, 0.0)
                    acc = acc + kern[o : o + 1, cs] * value
                    prod = own * value
                    part = prod[0:8]
                    for q in range(1, CHUNK // 8):
                        part = part + prod[8 * q : 8 * q + 8]
                    dkacc[o, :, cs] += part
                dglu[pl.ds(r0, CHUNK), cs] = acc

        flag = inside[micro, i]
        pl.when(flag > 0)(functools.partial(run, False))
        pl.when(flag == 0)(functools.partial(run, True))
        return carry

    lax.fori_loop(0, size // CHUNK, step, 0)
    dk[...] = jnp.sum(dkacc[...], axis=1)
    grad = dglu[...]
    g1 = (grad * p1[0].astype(F32)).astype(BF16)
    g2 = (grad * p2[0].astype(F32)).astype(BF16)
    dg[0, :, :512] = g1
    dg[0, :, 512:] = g2
    da = dot_nt(g1, w[:, :512]) + dot_nt(g2, w[:, 512:])
    n3, inv3 = norm(x2[0])
    sums[0, 0:1] = column_sum(da * n3)
    sums[0, 1:8] = jnp.zeros((7, D), F32)
    result = dx3[0] + norm_back(da, n3, inv3, gain_c)
    dx2[0] = result
    e2[0] = result.astype(BF16)


def attend_back_kernel(
    idx, x1, gain, cos, sin, dx2, q, k, v, pr, jm, jn, jf, om, on, of,
    dj, dx1, e1, sums, wj, wo, dmix, dq, dkey, sem,
):
    @pl.when(pl.program_id(0) == 0)
    def _():
        fetch(idx, ((jm, jn, jf), (om, on, of)), (wj, wo), sem)

    grad2 = dx2[0]
    dmix[...] = dot_nt(grad2.astype(BF16), wo[...]).astype(BF16)
    masks = head_masks()

    def pair(p, carry):
        c = pl.ds(pl.multiple_of(p * 128, 128), 128)
        qp, kp, vp, gp = q[0, :, c], k[0, :, c], v[0, :, c], dmix[:, c]
        parts = [None, None, None]
        for e in range(2):
            prob = pr[0, 2 * p + e]
            grad = gp * masks[e]
            dp = dot_nt(grad, vp)
            wide = prob.astype(F32)
            prod = wide * dp
            ds = (prod - wide * jnp.sum(prod, axis=-1, keepdims=True)).astype(BF16)
            new = (dot(ds, kp * masks[e]), dot_tn(ds, qp * masks[e]), dot_tn(prob, grad))
            parts = [b if a is None else a + b for a, b in zip(parts, new)]
        dq[:, c] = parts[0]
        dkey[:, c] = parts[1]
        dj[0, :, pl.ds(pl.multiple_of(1024 + p * 128, 128), 128)] = parts[2].astype(BF16)
        return carry

    lax.fori_loop(0, HEADS // 2, pair, 0)
    cosine, sine = cos[0], -sin[0]
    dj[0, :, :512] = turn(dq[...] * HDIM ** (-0.5), cosine, sine).astype(BF16)
    dj[0, :, 512:1024] = turn(dkey[...], cosine, sine).astype(BF16)
    da = dot_nt(dj[0], wj[...])
    n2, inv2 = norm(x1[0])
    sums[0, 0:1] = column_sum(da * n2)
    sums[0, 1:8] = jnp.zeros((7, D), F32)
    out = grad2 + norm_back(da, n2, inv2, gain[...])
    dx1[0] = out
    e1[0] = (0.5 * out).astype(BF16)


def feed_back_kernel(idx, x, gain, dx1, e1, g1, um, un, uf, dm, dn, df, fg, dz, sums, u, d, sem):
    @pl.when(pl.program_id(0) == 0)
    def _():
        fetch(idx, ((um, un, uf), (dm, dn, df)), (u, d), sem)
        sums[...] = jnp.zeros(sums.shape, F32)

    e = e1[...]
    acc = None
    for j in range(4):
        c = slice(j * 512, (j + 1) * 512)
        g = (dot_nt(e, d[c, :]) * g1[:, c].astype(F32)).astype(BF16)
        dz[:, c] = g
        part = dot_nt(g, u[:, c])
        acc = part if acc is None else acc + part
    n1, inv1 = norm(x[...].astype(F32))
    sums[0:1] += column_sum(acc * n1)
    fg[...] = (dx1[...] + norm_back(acc, n1, inv1, gain[...])).astype(BF16)


def weight_kernel(plan, core, *refs):
    ins, (send, keep) = refs[:-2], refs[-2:]
    step = pl.program_id(0)

    def fill(out):
        at = 0
        for i, blocks in enumerate(plan):
            l0, r0, l1, r1 = ins[4 * i : 4 * i + 4]
            rows = l0.shape[1]
            for j in range(blocks):
                c = slice(j * 512, (j + 1) * 512)
                out[0, at : at + rows] = (
                    dot_tn(l0[...], r0[:, c]) + dot_tn(l1[...], r1[:, c])
                ).astype(BF16)
                at += rows

    @pl.when(step < 2)
    def _():
        fill(send)

    @pl.when(step >= 2)
    def _():
        fill(keep)


def full(shape):
    zeros = (0,) * len(shape)
    return pl.BlockSpec(shape, lambda *_: zeros)


def out(shape, dtype):
    return jax.ShapeDtypeStruct(shape, dtype)


def cost(flops, nbytes):
    return pl.CostEstimate(flops=int(flops), bytes_accessed=int(nbytes), transcendentals=0)


def micro_spec(shape, micro):
    rest = (0,) * len(shape)
    return pl.BlockSpec((1,) + shape, lambda *_: (micro,) + rest)


def weight_call(name, products, core, line, slots_of):
    plan, specs, arrays, rows, flops = [], [], [], 0, 0

    def quarter(step, core_ref):
        x = step % 2
        mine = core_ref[0]
        return x * 2 + jnp.where(step < 2, 1 - mine, mine)

    for lefts, rights in products:
        (l0, _), (r0, _) = lefts[0], rights[0]
        slots = slots_of
        m, n = l0.shape[1], r0.shape[1]
        plan.append(n // 512)
        rows += (n // 512) * (m // 4)
        flops += 4 * slots * m * n
        for (left, i), (right, j) in zip(lefts, rights):
            specs.append(pl.BlockSpec((slots, m // 4), lambda s, ref, i=i: (i, quarter(s, ref))))
            specs.append(pl.BlockSpec((slots, n), lambda s, ref, j=j: (j, 0)))
            arrays += [left, right]
    nbytes = sum(a.size * 2 for a in arrays) + rows * 512 * 8
    found = pl.pallas_call(
        functools.partial(weight_kernel, tuple(plan)),
        name=name,
        grid_spec=pltpu.PrefetchScalarGridSpec(
            num_scalar_prefetch=1,
            grid=(4,),
            in_specs=specs,
            out_specs=[
                pl.BlockSpec((1, rows, D), lambda s, ref: (jnp.minimum(s, 1), 0, 0)),
                pl.BlockSpec((1, rows, D), lambda s, ref: (jnp.maximum(s - 2, 0), 0, 0)),
            ],
        ),
        out_shape=[out((2, rows, D), BF16)] * 2,
        cost_estimate=cost(flops, nbytes),
    )(core, *arrays)
    line.did(found[0])
    return found


def layout(lengths, mask, slots):
    ends = jnp.cumsum(lengths, axis=1)
    starts = ends - lengths
    slot = jnp.arange(slots, dtype=jnp.int32)
    reached = slot[None, :, None] >= ends[:, None, :]
    segment = jnp.sum(reached.astype(jnp.int32), axis=2)
    member = segment[:, :, None] == jnp.arange(lengths.shape[1], dtype=jnp.int32)
    begin = jnp.sum(jnp.where(member, starts[:, None, :], 0), axis=2)
    end = jnp.sum(jnp.where(member, ends[:, None, :], 0), axis=2)
    return segment, slot[None] - begin, end - 1 - slot[None]


def body(
    sizes, frames, item_lengths, frame_mask, first_norm, first_up, first_down, attend_norm,
    attend_joint, attend_out, conv_norm, conv_in, conv_kern, batch_gain, batch_bias, conv_out,
    second_norm, second_up, second_down, final_norm, output_grad,
):
    slots = frames.shape[1]
    x_at = lax.axis_index("fsdp").astype(jnp.int32).reshape(1)
    core = (lax.axis_index("dp") & 1).astype(jnp.int32).reshape(1)
    first_x = lax.axis_index("fsdp") == 0

    where = jnp.concatenate([x_at, core])
    line = Line()

    norms = jnp.concatenate(
        [jnp.stack([first_norm, attend_norm, conv_norm, batch_gain, batch_bias, second_norm, final_norm]),
         jnp.zeros((1, D // 2), BF16), conv_kern.reshape(KER, D // 2)], axis=0
    )
    norms_o = swap(norms, "fsdp", 1, 2)
    names = ("up1", "down1", "joint", "aout", "cin", "cout", "up2", "down2")
    shards = dict(
        zip(
            names,
            (first_up, first_down, attend_joint, attend_out, conv_in, conv_out, second_up, second_down),
        )
    )
    pieces = {}
    for name in names:
        piece = shards[name].shape[0] // 2
        pieces[name] = lax.dynamic_slice_in_dim(shards[name], core[0] * piece, piece, axis=0)
    near = {name: swap(pieces[name], "fsdp", 1, 2) for name in names}
    far = {}

    def pass_on(*group):
        for name in group:
            far[name] = swap(line.after(near[name]), "dp", 1, sizes["dp"])

    def whole(name):
        return shards[name], near[name], far[name]

    first, second = jnp.where(first_x, norms, norms_o), jnp.where(first_x, norms_o, norms)
    gains = jnp.concatenate([first[:7], second[:7]], axis=1).astype(F32)
    kern = jnp.concatenate(
        [first[8:].reshape(KER // 2, D), second[8:].reshape(KER // 2, D)], axis=0
    ).astype(F32)
    segment, position, left = layout(item_lengths[:, 0], frame_mask, slots)
    half = HDIM // 2
    freq = jnp.exp(jnp.arange(half, dtype=F32) * (-2.0 * math.log(10000.0) / HDIM))
    angle = position.astype(F32)[:, :, None] * freq
    cosine, sine = jnp.cos(angle), jnp.sin(angle)
    cos_t = jnp.concatenate([cosine] * 4, axis=-1)
    sin_t = jnp.concatenate([-sine, sine, -sine, sine], axis=-1)
    valid = frame_mask.astype(F32)

    def wide(values):
        return jnp.broadcast_to(values.astype(F32)[:, :, None], (MB, slots, 128))

    segb, before, after, validb = wide(segment), wide(position), wide(left), wide(valid)
    rows = jnp.stack([segment.astype(F32), valid], axis=1)
    near_end = jnp.minimum(position, left).reshape(MB, slots // CHUNK, CHUNK)
    inside = (jnp.min(near_end, axis=2) >= PAD).astype(jnp.int32)

    tables = (gains, kern, cos_t, sin_t, segb, before, after, validb, rows, inside)
    tables = lax.optimization_barrier(tables)
    gains, kern, cos_t, sin_t, segb, before, after, validb, rows, inside = tables
    g_first, g_attend, g_conv, g_bn, b_bn, g_second, g_final = (gains[i : i + 1] for i in range(7))
    line.did(gains, *pieces.values())
    pass_on("up1", "down1")

    tall = MB * slots
    tm = 256
    x_flat = frames.reshape(tall, D)

    def row_spec(width):
        return pl.BlockSpec((tm, width), lambda i: (i, 0))

    x1, a1, h1, g1 = pl.pallas_call(
        feed_kernel,
        name="feed",
        grid=(tall // tm,),
        in_specs=[SMEM, row_spec(D), full((1, D)), *[ANY] * 6],
        out_specs=[row_spec(D), row_spec(D), row_spec(FF), row_spec(FF)],
        out_shape=[out((tall, D), F32), out((tall, D), BF16)] + [out((tall, FF), BF16)] * 2,
        scratch_shapes=weight_scratch((D, FF), (FF, D)),
        cost_estimate=cost(4 * tall * D * FF, 2e7),
    )(line.after(where), x_flat, g_first, *whole("up1"), *whole("down1"))
    line.did(a1)
    pass_on("joint", "aout")

    def cut(array):
        return array.reshape(MB, slots, array.shape[-1])

    def by_micro(*shape):
        rest = (0,) * len(shape)
        return pl.BlockSpec((1,) + shape, lambda i: (i,) + rest)

    x1 = cut(x1)
    x2, a2, qh, kh, vh, probs, mixed = pl.pallas_call(
        attend_kernel,
        name="attend",
        grid=(MB,),
        in_specs=[
            SMEM, by_micro(slots, D), full((1, D)), by_micro(slots, 128), by_micro(slots, 128),
            by_micro(slots, 128), by_micro(2, slots), *[ANY] * 6,
        ],
        out_specs=[by_micro(slots, D)] * 5 + [by_micro(HEADS, slots, slots), by_micro(slots, D)],
        out_shape=[out((MB, slots, D), F32)] + [out((MB, slots, D), BF16)] * 4
        + [out((MB, HEADS, slots, slots), BF16), out((MB, slots, D), BF16)],
        scratch_shapes=[
            pltpu.VMEM((D, 3 * D), BF16), pltpu.VMEM((D, D), BF16), pltpu.VMEM((slots, slots), F32),
            pltpu.SemaphoreType.DMA((6,)),
        ],
        cost_estimate=cost(MB * slots * (8 * D * D + 8 * slots * D), 3e7),
    )(line.after(where), x1, g_attend, cos_t, sin_t, segb, rows, *whole("joint"), *whole("aout"))
    line.did(a2)
    pass_on("cin")

    pad_rows = slots + 40

    tables_spec = [by_micro(slots, 128)] * 3
    a3, glu, p1, p2, conv, stats = pl.pallas_call(
        conv_kernel,
        name="conv",
        grid=(MB,),
        in_specs=[
            SMEM, SMEM, by_micro(slots, D), full((1, D)), full((KER, D)), *tables_spec, *[ANY] * 3,
        ],
        out_specs=[by_micro(slots, D)] * 5 + [by_micro(4, D)],
        out_shape=[
            out((MB, slots, D), BF16), out((MB, slots, D), F32), out((MB, slots, D), BF16),
            out((MB, slots, D), BF16), out((MB, slots, D), F32), out((MB, 4, D), F32),
        ],
        scratch_shapes=[
            pltpu.VMEM((D, 2 * D), BF16), pltpu.VMEM((pad_rows, D), F32),
            pltpu.VMEM((8, pad_rows - 8, D), F32), pltpu.SemaphoreType.DMA((3,)),
        ],
        cost_estimate=cost(MB * (4 * slots * D * D + 60 * KER * slots * D), 2e7),
    )(line.after(where), inside, x2, g_conv, kern, validb, before, after, *whole("cin"))
    stats = stats.reshape(4 * MB, D)
    line.did(stats)
    pass_on("cout", "up2", "down2")
    sync = Sum(line, sizes, stats)
    while sync.step():
        pass
    total = sync.value.reshape(MB, 4, D)
    mid_gains = jnp.concatenate([g_bn, b_bn, g_second, g_final], axis=0)
    tiles = slots // tm

    def tile_spec(width):
        return pl.BlockSpec((tm, width), lambda m, i: (m * tiles + i, 0))

    def per_micro(rows_of):
        return pl.BlockSpec((1, rows_of, D), lambda m, *_: (m, 0, 0))

    enc, a4, e3, a5, h2, dz2, e4, db, dx3, mid_sums = pl.pallas_call(
        middle_kernel,
        name="middle",
        grid=(MB, tiles),
        in_specs=[SMEM, per_micro(4), full((4, D)), *[tile_spec(D)] * 3, *[ANY] * 9],
        out_specs=[tile_spec(D)] * 4 + [tile_spec(FF)] * 2 + [tile_spec(D)] * 3 + [per_micro(8)],
        out_shape=[out((tall, D), BF16)] * 4 + [out((tall, FF), BF16)] * 2
        + [out((tall, D), BF16)] + [out((tall, D), F32)] * 2 + [out((MB, 8, D), F32)],
        scratch_shapes=[
            pltpu.VMEM((D, D), BF16), pltpu.VMEM((D, FF), BF16), pltpu.VMEM((FF, D), BF16),
            pltpu.VMEM((tm, FF), BF16), pltpu.SemaphoreType.DMA((9,)),
        ],
        cost_estimate=cost(tall * (8 * D * FF + 4 * D * D), 4e7),
    )(line.after(where), total, mid_gains, conv.reshape(tall, D), x2.reshape(tall, D),
      output_grad.reshape(tall, D), *whole("cout"), *whole("up2"), *whole("down2"))
    stats = mid_sums[:, :2].reshape(2 * MB, D)
    line.did(stats)
    sync = Sum(line, sizes, stats)

    def product(*sides):
        found = []
        for side in sides:
            if isinstance(side, list):
                found.append([(array, 0) for array in side])
            else:
                found.append([(side.reshape(tall, side.shape[-1]), m) for m in range(MB)])
        return found

    def weights(name, *products):
        return weight_call(name, products, line.after(core), line, slots)

    pair = weights("weights_second", product(h2, e4), product(a5, dz2), product(a4, e3))
    chain_a = Background(line, sizes, ((FF, D), (D, FF), (D, D)), *pair)
    while sync.step():
        pass
    chain_a.step()
    back = sync.value.reshape(MB, 2, D)
    back_gains = jnp.concatenate([g_bn, g_conv], axis=0)
    dg, dx2, e2, kern_sum, sums_conv = pl.pallas_call(
        conv_back_kernel,
        name="conv_back",
        grid=(MB,),
        in_specs=[
            SMEM, SMEM, per_micro(4), per_micro(2), full((2, D)), full((KER, D)),
            *[by_micro(slots, D)] * 7, *tables_spec, *[ANY] * 3,
        ],
        out_specs=[
            by_micro(slots, 2 * D), by_micro(slots, D), by_micro(slots, D), full((KER, D)), per_micro(8),
        ],
        out_shape=[
            out((MB, slots, 2 * D), BF16), out((MB, slots, D), F32), out((MB, slots, D), BF16),
            out((KER, D), F32), out((MB, 8, D), F32),
        ],
        scratch_shapes=[
            pltpu.VMEM((D, 2 * D), BF16), pltpu.VMEM((pad_rows, D), F32),
            pltpu.VMEM((8, pad_rows - 8, D), F32), pltpu.VMEM((slots, D), F32),
            pltpu.VMEM((KER, 8, D), F32), pltpu.SemaphoreType.DMA((3,)),
        ],
        cost_estimate=cost(MB * (4 * slots * D * D + 120 * KER * slots * D), 3e7),
    )(line.after(where), inside, total, back, back_gains, kern, conv, cut(db), glu, p1, p2, x2, cut(dx3),
      validb, before, after, *whole("cin"))
    line.did(sums_conv)
    pair = weights("weights_conv", product(a3, dg), product(mixed, e2))
    chain_c = Background(line, sizes, ((D, 2 * D), (D, D)), *pair)
    chain_a.step()
    chain_c.step()

    dj, dx1, e1, sums_attend = pl.pallas_call(
        attend_back_kernel,
        name="attend_back",
        grid=(MB,),
        in_specs=[
            SMEM, by_micro(slots, D), full((1, D)), *[by_micro(slots, 128)] * 2,
            *[by_micro(slots, D)] * 4, by_micro(HEADS, slots, slots), *[ANY] * 6,
        ],
        out_specs=[by_micro(slots, 3 * D), by_micro(slots, D), by_micro(slots, D), by_micro(8, D)],
        out_shape=[
            out((MB, slots, 3 * D), BF16), out((MB, slots, D), F32), out((MB, slots, D), BF16),
            out((MB, 8, D), F32),
        ],
        scratch_shapes=[
            pltpu.VMEM((D, 3 * D), BF16), pltpu.VMEM((D, D), BF16), pltpu.VMEM((slots, D), BF16),
            pltpu.VMEM((slots, D), F32), pltpu.VMEM((slots, D), F32), pltpu.SemaphoreType.DMA((6,)),
        ],
        cost_estimate=cost(MB * slots * (8 * D * D + 16 * slots * D), 3e7),
    )(line.after(where), x1, g_attend, cos_t, sin_t, dx2, qh, kh, vh, probs,
      *whole("joint"), *whole("aout"))
    line.did(sums_attend)
    chain_c.step()
    reduce_behind((chain_a, chain_c), sizes["dp"])
    pair = weights("weights_down", product(h1, e1), product(a2, dj))
    chain_d = Chain(line, sizes, ((FF, D), (D, 3 * D)), *pair, 3)
    dx1, e1 = dx1.reshape(tall, D), e1.reshape(tall, D)

    def back_feed(m):
        def at_micro(width):
            return pl.BlockSpec((tm, width), lambda i: (m * tiles + i, 0))

        found = pl.pallas_call(
            feed_back_kernel,
            name=f"feed_back_{m}",
            grid=(tiles,),
            in_specs=[
                SMEM, at_micro(D), full((1, D)), at_micro(D), at_micro(D), at_micro(FF), *[ANY] * 6,
            ],
            out_specs=[row_spec(D), row_spec(FF), full((8, D))],
            out_shape=[out((slots, D), BF16), out((slots, FF), BF16), out((8, D), F32)],
            scratch_shapes=weight_scratch((D, FF), (FF, D)),
            cost_estimate=cost(4 * slots * D * FF, 1e7),
        )(line.after(where), x_flat, g_first, dx1, e1, g1, *whole("up1"), *whole("down1"))
        line.did(found[2])
        return found

    feed_backs = [back_feed(0)]
    chain_d.step()
    feed_backs.append(back_feed(1))
    pair = weights("weights_up", product(a1, [f[1] for f in feed_backs]))
    chain_f = Chain(line, sizes, ((D, FF),), *pair, 1)

    mid_sums = mid_sums[0] + mid_sums[1]
    small = jnp.concatenate(
        [
            kern_sum,
            feed_backs[0][2][0:1] + feed_backs[1][2][0:1],
            sums_attend[0, 0:1] + sums_attend[1, 0:1],
            sums_conv[0, 0:1] + sums_conv[1, 0:1],
            mid_sums[1:2],
            mid_sums[0:1],
            mid_sums[2:4],
            jnp.zeros((1, D), F32),
        ],
        axis=0,
    )
    line.did(small)
    small = Sum(line, sizes, small)
    chain_d.step()
    chain_f.step()
    small.step()
    small.step()
    chain_d.step()
    small.step()
    chain_f.step()
    chain_d.step()
    small.step()
    chain_f.step()
    chain_d.step()
    chain_f.step()
    small.step()
    chain_a.pass_on()
    chain_d.step()
    chain_f.step()
    chain_a.step()
    chain_c.pass_on()
    chain_d.step()
    chain_f.step()
    chain_c.step()
    chain_d.step()
    chain_f.step()
    for chain in (chain_d, chain_f):
        while chain.plan:
            chain.step()
    while small.plan:
        small.step()
    small = small.value
    kern_grad = lax.dynamic_slice_in_dim(small, x_at[0] * (KER // 2), KER // 2, axis=0)
    vectors = lax.dynamic_slice_in_dim(small[KER:], x_at[0] * (D // 2), D // 2, axis=1)
    down2_g, up2_g, cout_g = chain_a.result
    cin_g, aout_g = chain_c.result
    down1_g, joint_g = chain_d.result
    (up1_g,) = chain_f.result
    fgrad = jnp.stack([f[0] for f in feed_backs])
    return (
        enc.reshape(MB, slots, D), fgrad, vectors[0], up1_g, down1_g, vectors[1], joint_g, aout_g,
        vectors[2], cin_g, kern_grad, vectors[3], vectors[4], cout_g, vectors[5], up2_g, down2_g,
        vectors[6],
    )


def solution(mesh):
    split = P(None, ("dp", "fsdp"), None)
    row, mat = P("fsdp"), P("fsdp", None)
    weights = (row, mat, mat, row, mat, mat, row, mat, mat, row, row, mat, row, mat, mat, row)
    return jax.shard_map(
        functools.partial(body, dict(mesh.shape)),
        mesh=mesh,
        in_specs=(split, split, P(None, ("dp", "fsdp"))) + weights + (split,),
        out_specs=(split, split) + weights,
        check_vma=False,
    )
```

```python
import functools
import math

import jax
import jax.numpy as jnp
from jax import lax
from jax.experimental import pallas as pl
from jax.experimental.pallas import tpu as pltpu
from jax.sharding import PartitionSpec as P

HEADS = 8
KER = 32
HDIM = 64
MB = 2
D = 512
FF = 2048
EPS = 1e-05
PAD = 16
CHUNK = 32
F32 = jnp.float32
BF16 = jnp.bfloat16
ANY = pl.BlockSpec(memory_space=pl.ANY)
SMEM = pl.BlockSpec(memory_space=pltpu.SMEM)
VMEM = pl.BlockSpec(memory_space=pltpu.VMEM)


def swap(value, axis, bit, size):
    return lax.ppermute(value, axis, [(i, i ^ bit) for i in range(size)])


def bits_of(size):
    return [1 << i for i in range(size.bit_length() - 1)]


class Line:
    def __init__(self):
        self.last = ()

    def after(self, value):
        return lax.optimization_barrier((value, self.last))[0] if self.last else value

    def did(self, *values):
        self.last = values


def add_split(keep, got, index):
    parts = []
    for at in (index, 1 - index):
        left = lax.dynamic_index_in_dim(keep, at, 0, keepdims=False)
        right = lax.dynamic_index_in_dim(got, at, 0, keepdims=False)
        parts.append((left.astype(F32) + right.astype(F32)).astype(BF16))
    return parts


def unpack_kernel(shapes, index, keep, got, *outs):
    at = 0
    for (m, n), target in zip(shapes, outs):
        quarter = m // 4
        for source, core in ((keep, index[0]), (got, 1 - index[0])):
            rows = pl.ds(pl.multiple_of(core * quarter, quarter), quarter)
            for j in range(n // 512):
                first = at + j * quarter
                target[rows, j * 512 : (j + 1) * 512] = source[first : first + quarter].astype(F32)
        at += (n // 512) * quarter


class Chain:
    def __init__(self, line, sizes, shapes, got, keep, halved):
        self.line, self.sizes, self.shapes, self.keep = line, sizes, shapes, keep
        bits = bits_of(sizes["dp"])[1:]
        halved = bits[:halved]
        whole = bits[len(halved) :]
        self.plan = [("split", "x")] + [("split", bit) for bit in halved] + [("add", bit) for bit in whole]
        self.plan += [("last", None)] + [("join", bit) for bit in halved[::-1]] + [("unpack", 1)]
        self.order = ["x"] + halved + whole + halved[::-1] + [1]
        self.got = got
        self.result = None

    def where(self, bit):
        if bit == "x":
            return lax.axis_index("fsdp").astype(jnp.int32)
        return ((lax.axis_index("dp") & bit) > 0).astype(jnp.int32)

    def send(self, value):
        bit = self.order.pop(0)
        if bit == "x":
            self.got = swap(value, "fsdp", 1, 2)
        else:
            self.got = swap(value, "dp", bit, self.sizes["dp"])

    def step(self):
        kind, bit = self.plan.pop(0)
        got = self.line.after(self.got)
        keep = self.keep
        if kind == "split":
            rows = keep.size // (2 * D)
            self.keep, send = add_split(keep.reshape(2, rows, D), got.reshape(2, rows, D), self.where(bit))
            self.line.did(send, self.keep)
            self.send(send)
        elif kind in ("add", "last"):
            self.keep = (keep.astype(F32) + got.astype(F32)).astype(BF16)
            self.line.did(self.keep)
            self.send(self.keep)
        elif kind == "join":
            low = self.where(bit) == 0
            self.keep = jnp.concatenate([jnp.where(low, keep, got), jnp.where(low, got, keep)], axis=0)
            self.line.did(self.keep)
            self.send(self.keep)
        else:
            outs = [out((m // 2, n), F32) for m, n in self.shapes]
            self.result = pl.pallas_call(
                functools.partial(unpack_kernel, self.shapes),
                name="unpack",
                in_specs=[SMEM, VMEM, VMEM],
                out_specs=[VMEM] * len(outs),
                out_shape=outs,
                cost_estimate=cost(0, 12 * keep.size),
            )(self.where(1).reshape(1), keep, got)
            self.line.did(self.result[-1])


class Background(Chain):
    def __init__(self, line, sizes, shapes, got, keep):
        super().__init__(line, sizes, shapes, got, keep, 0)
        self.plan = [("split", "x"), ("total", None), ("unpack", 1)]

    def step(self):
        if self.plan[0][0] != "total":
            return super().step()
        self.plan.pop(0)
        got = self.line.after(self.got)
        self.keep = (self.keep.astype(F32) + got.astype(F32)).astype(BF16)
        self.line.did(self.keep)

    def pass_on(self):
        self.keep = self.line.after(self.keep)
        self.got = swap(self.keep, "dp", 1, self.sizes["dp"])


def reduce_behind(chains, size):
    groups = [[i for i in range(size) if i % 2 == c] for c in range(2)]
    totals = lax.psum(tuple(c.keep for c in chains), "dp", axis_index_groups=groups)
    for chain, total in zip(chains, totals):
        chain.keep = total


class Sum:
    def __init__(self, line, sizes, value, late=()):
        self.line, self.sizes, self.value = line, sizes, value
        bits = bits_of(sizes["dp"])
        self.plan = [bit for bit in bits if bit not in late] + list(late) + ["x"]
        self.start()

    def start(self):
        bit = self.plan.pop(0)
        if bit == "x":
            self.got = swap(self.value, "fsdp", 1, 2)
        else:
            self.got = swap(self.value, "dp", bit, self.sizes["dp"])

    def step(self):
        self.value = self.value + self.line.after(self.got)
        self.line.did(self.value)
        if self.plan:
            self.start()
            return True
        return False


def dot(left, right):
    return lax.dot_general(left, right, (((1,), (0,)), ((), ())), preferred_element_type=F32)


def dot_nt(left, right):
    return lax.dot_general(left, right, (((1,), (1,)), ((), ())), preferred_element_type=F32)


def dot_tn(left, right):
    return lax.dot_general(left, right, (((0,), (0,)), ((), ())), preferred_element_type=F32)


def sigmoid(values):
    return 0.5 * jnp.tanh(0.5 * values) + 0.5


def norm(values):
    centered = values - jnp.mean(values, axis=-1, keepdims=True)
    inverse = lax.rsqrt(jnp.mean(centered * centered, axis=-1, keepdims=True) + EPS)
    return centered * inverse, inverse


def norm_back(grad, rows, inverse, gain):
    scaled = grad * gain
    return inverse * (
        scaled
        - jnp.mean(scaled, axis=-1, keepdims=True)
        - rows * jnp.mean(scaled * rows, axis=-1, keepdims=True)
    )


def column_sum(values):
    return jnp.sum(values, axis=0, keepdims=True)


def fetch(where, sources, targets, sem):
    copies = []
    for i, (mine, near, far) in enumerate(sources):
        rows = mine.shape[0]
        piece = rows // 2
        start = (1 - where[0]) * rows
        places = (where[0] * rows, start + where[1] * piece, start + (1 - where[1]) * piece)
        for j, source in enumerate((mine, near, far)):
            at = pl.multiple_of(places[j], piece)
            copies.append(
                pltpu.make_async_copy(
                    source, targets[i].at[pl.ds(at, source.shape[0])], sem.at[3 * i + j]
                )
            )
    for copy in copies:
        copy.start()
    for copy in copies:
        copy.wait()


def weight_scratch(*shapes):
    return [pltpu.VMEM(shape, BF16) for shape in shapes] + [
        pltpu.SemaphoreType.DMA((3 * len(shapes),))
    ]


def tile4(values):
    return jnp.concatenate([values] * 4, axis=1)


def turn(values, cosine, sine):
    lane = lax.broadcasted_iota(jnp.int32, (values.shape[0], 128), 1)
    first = (lane & 63) < 32
    parts = []
    for c in range(4):
        u = values[:, c * 128 : (c + 1) * 128]
        swapped = jnp.where(first, pltpu.roll(u, 96, 1), pltpu.roll(u, 32, 1))
        parts.append(u * cosine + swapped * sine)
    return jnp.concatenate(parts, axis=1)


def head_masks():
    lane = lax.broadcasted_iota(jnp.int32, (1, 128), 1)
    return [((lane >> 6) == e).astype(F32).astype(BF16) for e in range(2)]


def feed_kernel(idx, x, gain, um, un, uf, dm, dn, df, x1, a1, h1, g1, u, d, sem):
    @pl.when(pl.program_id(0) == 0)
    def _():
        fetch(idx, ((um, un, uf), (dm, dn, df)), (u, d), sem)

    v = x[...].astype(F32)
    a = (norm(v)[0] * gain[...]).astype(BF16)
    a1[...] = a
    acc = None
    for j in range(4):
        c = slice(j * 512, (j + 1) * 512)
        z = dot(a, u[:, c])
        s = sigmoid(z)
        h = z * s
        g1[:, c] = (s + h * (1.0 - s)).astype(BF16)
        h = h.astype(BF16)
        h1[:, c] = h
        part = dot(h, d[c, :])
        acc = part if acc is None else acc + part
    x1[...] = v + 0.5 * acc


def attend_kernel(
    idx, x1, gain, cos, sin, segb, rows, jm, jn, jf, om, on, of,
    x2, a2, qo, ko, vo, pr, mixed, wj, wo, bias, sem,
):
    @pl.when(pl.program_id(0) == 0)
    def _():
        fetch(idx, ((jm, jn, jf), (om, on, of)), (wj, wo), sem)

    v = x1[0]
    a = (norm(v)[0] * gain[...]).astype(BF16)
    a2[0] = a
    cosine, sine = cos[0], sin[0]
    qo[0] = (turn(dot(a, wj[:, :512]), cosine, sine) * HDIM ** (-0.5)).astype(BF16)
    ko[0] = turn(dot(a, wj[:, 512:1024]), cosine, sine).astype(BF16)
    vo[0] = dot(a, wj[:, 1024:]).astype(BF16)
    size = bias.shape[0]
    row = lax.broadcasted_iota(jnp.int32, (size, size), 0)
    col = lax.broadcasted_iota(jnp.int32, (size, size), 1)
    allowed = (tile4(segb[0]) == rows[0, 0:1, :]) & ((rows[0, 1:2, :] > 0) | (row == col))
    bias[...] = jnp.where(allowed, 0.0, -1000000000.0)
    masks = head_masks()

    def pair(p, carry):
        c = pl.ds(pl.multiple_of(p * 128, 128), 128)
        q, k, val = qo[0, :, c], ko[0, :, c], vo[0, :, c]
        total = None
        for e in range(2):
            s = dot_nt(q * masks[e], k) + bias[...]
            ex = jnp.exp(s - jnp.max(s, axis=-1, keepdims=True))
            prob = (ex * (1.0 / jnp.sum(ex, axis=-1, keepdims=True))).astype(BF16)
            pr[0, 2 * p + e] = prob
            part = dot(prob, val * masks[e])
            total = part if total is None else total + part
        mixed[0, :, c] = total.astype(BF16)
        return carry

    lax.fori_loop(0, HEADS // 2, pair, 0)
    x2[0] = v + dot(mixed[0], wo[...])


def conv_taps(padded, shifts):
    rows = shifts.shape[1]
    for b in range(8):
        shifts[b] = padded[b : b + rows, :]


def conv_kernel(
    idx, inside, x2, gain, kern, validb, before, after, wm, wn, wf,
    a3, glu, p1, p2, cout, stats, w, padded, shifts, sem,
):
    micro = pl.program_id(0)
    size = x2.shape[1]

    @pl.when(micro == 0)
    def _():
        fetch(idx, ((wm, wn, wf),), (w,), sem)
        padded[0:PAD] = jnp.zeros((PAD, D), F32)
        padded[PAD + size :] = jnp.zeros((padded.shape[0] - PAD - size, D), F32)

    a = (norm(x2[0])[0] * gain[...]).astype(BF16)
    a3[0] = a
    valid = tile4(validb[0])
    g1 = dot(a, w[:, :512])
    s = sigmoid(dot(a, w[:, 512:])) * valid
    g = g1 * s
    glu[0] = g
    p1[0] = s.astype(BF16)
    p2[0] = (g * (1.0 - s)).astype(BF16)
    padded[PAD : PAD + size] = g
    conv_taps(padded, shifts)

    def step(i, carry):
        r0 = pl.multiple_of(i * CHUNK, CHUNK)

        def run(masked):
            if masked:
                low, high = before[0, pl.ds(r0, CHUNK), :], after[0, pl.ds(r0, CHUNK), :]
            acc = [jnp.zeros((CHUNK, 128), F32) for _ in range(4)]
            for o in range(KER):
                shift_by = o - (KER - 1) // 2
                a8, b = divmod(shift_by + PAD, 8)
                if masked and shift_by < 0:
                    keep = low >= float(-shift_by)
                elif masked and shift_by > 0:
                    keep = high >= float(shift_by)
                for c in range(4):
                    cs = slice(c * 128, (c + 1) * 128)
                    value = shifts[b, pl.ds(r0 + 8 * a8, CHUNK), cs]
                    if masked and shift_by != 0:
                        value = jnp.where(keep, value, 0.0)
                    acc[c] = acc[c] + kern[o : o + 1, cs] * value
            for c in range(4):
                cout[0, pl.ds(r0, CHUNK), c * 128 : (c + 1) * 128] = acc[c]

        flag = inside[micro, i]
        pl.when(flag > 0)(functools.partial(run, False))
        pl.when(flag == 0)(functools.partial(run, True))
        return carry

    lax.fori_loop(0, size // CHUNK, step, 0)
    result = cout[0]
    weighted = result * valid
    stats[0, 0:1] = column_sum(weighted)
    stats[0, 1:2] = column_sum(weighted * result)
    stats[0, 2:3] = column_sum(valid)
    stats[0, 3:4] = jnp.zeros((1, D), F32)


def middle_kernel(
    idx, total, gains, conv, x2, og, cm, cn, cf, um, un, uf, dm, dn, df,
    enc, a4, e3, a5, h2, dz, e4, db, dx3, sums, wc, u, d, deriv, sem,
):
    @pl.when((pl.program_id(0) == 0) & (pl.program_id(1) == 0))
    def _():
        fetch(idx, ((cm, cn, cf), (um, un, uf), (dm, dn, df)), (wc, u, d), sem)

    @pl.when(pl.program_id(1) == 0)
    def _():
        sums[...] = jnp.zeros(sums.shape, F32)

    gain_b, bias_b, gain_2, gain_f = (gains[i : i + 1] for i in range(4))
    count = total[0, 2:3]
    mean = total[0, 0:1] / count
    inverse = lax.rsqrt(total[0, 1:2] / count - mean * mean + EPS)
    unit = (conv[...] - mean) * inverse
    act = unit * gain_b + bias_b
    s_act = sigmoid(act)
    a = (act * s_act).astype(BF16)
    a4[...] = a
    v3 = x2[...] + dot(a, wc[...])
    n5, inv5 = norm(v3)
    a = (n5 * gain_2).astype(BF16)
    a5[...] = a
    acc = None
    for j in range(4):
        c = slice(j * 512, (j + 1) * 512)
        z = dot(a, u[:, c])
        s = sigmoid(z)
        h = z * s
        deriv[:, c] = (s + h * (1.0 - s)).astype(BF16)
        h = h.astype(BF16)
        h2[:, c] = h
        part = dot(h, d[c, :])
        acc = part if acc is None else acc + part
    n6, inv6 = norm(v3 + 0.5 * acc)
    enc[...] = (n6 * gain_f).astype(BF16)
    dy = og[...].astype(F32)
    sums[0, 3:4] += column_sum(dy * n6)
    grad4 = norm_back(dy, n6, inv6, gain_f)
    e = (0.5 * grad4).astype(BF16)
    e4[...] = e
    acc = None
    for j in range(4):
        c = slice(j * 512, (j + 1) * 512)
        g = (dot_nt(e, d[c, :]) * deriv[:, c].astype(F32)).astype(BF16)
        dz[:, c] = g
        part = dot_nt(g, u[:, c])
        acc = part if acc is None else acc + part
    sums[0, 2:3] += column_sum(acc * n5)
    grad3 = grad4 + norm_back(acc, n5, inv5, gain_2)
    dx3[...] = grad3
    e = grad3.astype(BF16)
    e3[...] = e
    dact = dot_nt(e, wc[...]) * (s_act * (1.0 + act * (1.0 - s_act)))
    db[...] = dact
    sums[0, 0:1] += column_sum(dact)
    sums[0, 1:2] += column_sum(dact * unit)


def conv_back_kernel(
    idx, inside, total, back, gains, kern, conv, db, glu, p1, p2, x2, dx3, validb, before, after, wm, wn, wf,
    dg, dx2, e2, dk, sums, w, padded, shifts, dglu, dkacc, sem,
):
    micro = pl.program_id(0)
    size = x2.shape[1]

    @pl.when(micro == 0)
    def _():
        fetch(idx, ((wm, wn, wf),), (w,), sem)
        padded[0:PAD] = jnp.zeros((PAD, D), F32)
        padded[PAD + size :] = jnp.zeros((padded.shape[0] - PAD - size, D), F32)
        dkacc[...] = jnp.zeros(dkacc.shape, F32)

    gain_b, gain_c = gains[0:1], gains[1:2]
    count = total[0, 2:3]
    mean = total[0, 0:1] / count
    inverse = lax.rsqrt(total[0, 1:2] / count - mean * mean + EPS)
    share = inverse / count
    at_one, at_unit = share * (gain_b * back[0, 0:1]), share * (gain_b * back[0, 1:2])
    unit = (conv[0] - mean) * inverse
    padded[PAD : PAD + size] = db[0] * (inverse * gain_b) - tile4(validb[0]) * (at_one + unit * at_unit)
    conv_taps(padded, shifts)

    def step(i, carry):
        r0 = pl.multiple_of(i * CHUNK, CHUNK)

        def run(masked):
            if masked:
                low, high = before[0, pl.ds(r0, CHUNK), :], after[0, pl.ds(r0, CHUNK), :]
            for c in range(4):
                cs = slice(c * 128, (c + 1) * 128)
                own = glu[0, pl.ds(r0, CHUNK), cs]
                acc = jnp.zeros((CHUNK, 128), F32)
                for o in range(KER):
                    shift_by = (KER - 1) // 2 - o
                    a8, b = divmod(shift_by + PAD, 8)
                    value = shifts[b, pl.ds(r0 + 8 * a8, CHUNK), cs]
                    if masked and shift_by < 0:
                        value = jnp.where(low >= float(-shift_by), value, 0.0)
                    elif masked and shift_by > 0:
                        value = jnp.where(high >= float(shift_by), value, 0.0)
                    acc = acc + kern[o : o + 1, cs] * value
                    prod = own * value
                    part = prod[0:8]
                    for q in range(1, CHUNK // 8):
                        part = part + prod[8 * q : 8 * q + 8]
                    dkacc[o, :, cs] += part
                dglu[pl.ds(r0, CHUNK), cs] = acc

        flag = inside[micro, i]
        pl.when(flag > 0)(functools.partial(run, False))
        pl.when(flag == 0)(functools.partial(run, True))
        return carry

    lax.fori_loop(0, size // CHUNK, step, 0)
    dk[...] = jnp.sum(dkacc[...], axis=1)
    grad = dglu[...]
    g1 = (grad * p1[0].astype(F32)).astype(BF16)
    g2 = (grad * p2[0].astype(F32)).astype(BF16)
    dg[0, :, :512] = g1
    dg[0, :, 512:] = g2
    da = dot_nt(g1, w[:, :512]) + dot_nt(g2, w[:, 512:])
    n3, inv3 = norm(x2[0])
    sums[0, 0:1] = column_sum(da * n3)
    sums[0, 1:8] = jnp.zeros((7, D), F32)
    result = dx3[0] + norm_back(da, n3, inv3, gain_c)
    dx2[0] = result
    e2[0] = result.astype(BF16)


def attend_back_kernel(
    idx, x1, gain, cos, sin, dx2, q, k, v, pr, jm, jn, jf, om, on, of,
    dj, dx1, e1, sums, wj, wo, dmix, dq, dkey, sem,
):
    @pl.when(pl.program_id(0) == 0)
    def _():
        fetch(idx, ((jm, jn, jf), (om, on, of)), (wj, wo), sem)

    grad2 = dx2[0]
    dmix[...] = dot_nt(grad2.astype(BF16), wo[...]).astype(BF16)
    masks = head_masks()

    def pair(p, carry):
        c = pl.ds(pl.multiple_of(p * 128, 128), 128)
        qp, kp, vp, gp = q[0, :, c], k[0, :, c], v[0, :, c], dmix[:, c]
        parts = [None, None, None]
        for e in range(2):
            prob = pr[0, 2 * p + e]
            grad = gp * masks[e]
            dp = dot_nt(grad, vp)
            wide = prob.astype(F32)
            prod = wide * dp
            ds = (prod - wide * jnp.sum(prod, axis=-1, keepdims=True)).astype(BF16)
            new = (dot(ds, kp * masks[e]), dot_tn(ds, qp * masks[e]), dot_tn(prob, grad))
            parts = [b if a is None else a + b for a, b in zip(parts, new)]
        dq[:, c] = parts[0]
        dkey[:, c] = parts[1]
        dj[0, :, pl.ds(pl.multiple_of(1024 + p * 128, 128), 128)] = parts[2].astype(BF16)
        return carry

    lax.fori_loop(0, HEADS // 2, pair, 0)
    cosine, sine = cos[0], -sin[0]
    dj[0, :, :512] = turn(dq[...] * HDIM ** (-0.5), cosine, sine).astype(BF16)
    dj[0, :, 512:1024] = turn(dkey[...], cosine, sine).astype(BF16)
    da = dot_nt(dj[0], wj[...])
    n2, inv2 = norm(x1[0])
    sums[0, 0:1] = column_sum(da * n2)
    sums[0, 1:8] = jnp.zeros((7, D), F32)
    out = grad2 + norm_back(da, n2, inv2, gain[...])
    dx1[0] = out
    e1[0] = (0.5 * out).astype(BF16)


def feed_back_kernel(idx, x, gain, dx1, e1, g1, um, un, uf, dm, dn, df, fg, dz, sums, u, d, sem):
    @pl.when(pl.program_id(0) == 0)
    def _():
        fetch(idx, ((um, un, uf), (dm, dn, df)), (u, d), sem)
        sums[...] = jnp.zeros(sums.shape, F32)

    e = e1[...]
    acc = None
    for j in range(4):
        c = slice(j * 512, (j + 1) * 512)
        g = (dot_nt(e, d[c, :]) * g1[:, c].astype(F32)).astype(BF16)
        dz[:, c] = g
        part = dot_nt(g, u[:, c])
        acc = part if acc is None else acc + part
    n1, inv1 = norm(x[...].astype(F32))
    sums[0:1] += column_sum(acc * n1)
    fg[...] = (dx1[...] + norm_back(acc, n1, inv1, gain[...])).astype(BF16)


def weight_kernel(plan, core, *refs):
    ins, result = refs[:-1], refs[-1]
    at = 0
    for i, blocks in enumerate(plan):
        l0, r0, l1, r1 = ins[4 * i : 4 * i + 4]
        rows = l0.shape[1]
        for j in range(blocks):
            c = slice(j * 512, (j + 1) * 512)
            result[0, at : at + rows] = (
                dot_tn(l0[...], r0[:, c]) + dot_tn(l1[...], r1[:, c])
            ).astype(BF16)
            at += rows


def full(shape):
    zeros = (0,) * len(shape)
    return pl.BlockSpec(shape, lambda *_: zeros)


def out(shape, dtype):
    return jax.ShapeDtypeStruct(shape, dtype)


def cost(flops, nbytes):
    return pl.CostEstimate(flops=int(flops), bytes_accessed=int(nbytes), transcendentals=0)


def micro_spec(shape, micro):
    rest = (0,) * len(shape)
    return pl.BlockSpec((1,) + shape, lambda *_: (micro,) + rest)


def weight_call(name, products, core, line, slots_of):
    plan, specs, arrays, rows, flops = [], [], [], 0, 0

    def quarter(step, core_ref):
        return step * 2 + core_ref[0]

    for lefts, rights in products:
        (l0, _), (r0, _) = lefts[0], rights[0]
        slots = slots_of
        m, n = l0.shape[1], r0.shape[1]
        plan.append(n // 512)
        rows += (n // 512) * (m // 4)
        flops += 2 * slots * m * n
        for (left, i), (right, j) in zip(lefts, rights):
            specs.append(pl.BlockSpec((slots, m // 4), lambda s, ref, i=i: (i, quarter(s, ref))))
            specs.append(pl.BlockSpec((slots, n), lambda s, ref, j=j: (j, 0)))
            arrays += [left, right]
    nbytes = sum(a.size * 2 for a in arrays) + rows * 512 * 8
    found = pl.pallas_call(
        functools.partial(weight_kernel, tuple(plan)),
        name=name,
        grid_spec=pltpu.PrefetchScalarGridSpec(
            num_scalar_prefetch=1,
            grid=(2,),
            in_specs=specs,
            out_specs=pl.BlockSpec((1, rows, D), lambda s, ref: (s, 0, 0)),
        ),
        out_shape=out((2, rows, D), BF16),
        cost_estimate=cost(flops, nbytes),
    )(core, *arrays)
    line.did(found)
    return found


def layout(lengths, mask, slots):
    ends = jnp.cumsum(lengths, axis=1)
    starts = ends - lengths
    slot = jnp.arange(slots, dtype=jnp.int32)
    reached = slot[None, :, None] >= ends[:, None, :]
    segment = jnp.sum(reached.astype(jnp.int32), axis=2)
    member = segment[:, :, None] == jnp.arange(lengths.shape[1], dtype=jnp.int32)
    begin = jnp.sum(jnp.where(member, starts[:, None, :], 0), axis=2)
    end = jnp.sum(jnp.where(member, ends[:, None, :], 0), axis=2)
    return segment, slot[None] - begin, end - 1 - slot[None]


def body(
    sizes, frames, item_lengths, frame_mask, first_norm, first_up, first_down, attend_norm,
    attend_joint, attend_out, conv_norm, conv_in, conv_kern, batch_gain, batch_bias, conv_out,
    second_norm, second_up, second_down, final_norm, output_grad,
):
    slots = frames.shape[1]
    x_at = lax.axis_index("fsdp").astype(jnp.int32).reshape(1)
    core = (lax.axis_index("dp") & 1).astype(jnp.int32).reshape(1)
    first_x = lax.axis_index("fsdp") == 0

    where = jnp.concatenate([x_at, core])
    line = Line()

    names = ("up1", "down1", "joint", "aout", "cin", "cout", "up2", "down2")
    shards = dict(
        zip(
            names,
            (first_up, first_down, attend_joint, attend_out, conv_in, conv_out, second_up, second_down),
        )
    )
    pieces = {}

    def cut_piece(name):
        piece = shards[name].shape[0] // 2
        pieces[name] = lax.dynamic_slice_in_dim(shards[name], core[0] * piece, piece, axis=0)

    cut_piece("up1")
    cut_piece("down1")
    line.did(pieces["up1"], pieces["down1"])
    vectors = (first_norm, attend_norm, conv_norm, batch_gain, batch_bias, second_norm, final_norm)
    vectors, conv_kern = line.after((vectors, conv_kern))
    norms = jnp.concatenate(
        [jnp.stack(vectors), jnp.zeros((1, D // 2), BF16), conv_kern.reshape(KER, D // 2)], axis=0
    )
    for name in names[2:]:
        cut_piece(name)
    near = {name: swap(pieces[name], "fsdp", 1, 2) for name in names[:2]}
    norms_o = swap(norms, "fsdp", 1, 2)
    near |= {name: swap(pieces[name], "fsdp", 1, 2) for name in names[2:]}
    far = {}

    def pass_on(*group):
        for name in group:
            far[name] = swap(line.after(near[name]), "dp", 1, sizes["dp"])

    def whole(name):
        return shards[name], near[name], far[name]

    segment, position, left = layout(item_lengths[:, 0], frame_mask, slots)
    half = HDIM // 2
    freq = jnp.exp(jnp.arange(half, dtype=F32) * (-2.0 * math.log(10000.0) / HDIM))
    angle = position.astype(F32)[:, :, None] * freq
    cosine, sine = jnp.cos(angle), jnp.sin(angle)
    cos_t = jnp.concatenate([cosine] * 4, axis=-1)
    sin_t = jnp.concatenate([-sine, sine, -sine, sine], axis=-1)
    valid = frame_mask.astype(F32)

    def wide(values):
        return jnp.broadcast_to(values.astype(F32)[:, :, None], (MB, slots, 128))

    segb, before, after, validb = wide(segment), wide(position), wide(left), wide(valid)
    rows = jnp.stack([segment.astype(F32), valid], axis=1)
    near_end = jnp.minimum(position, left).reshape(MB, slots // CHUNK, CHUNK)
    inside = (jnp.min(near_end, axis=2) >= PAD).astype(jnp.int32)

    tables = (cos_t, sin_t, segb, before, after, validb, rows, inside)
    tables = lax.optimization_barrier((tables, tuple(pieces.values())))[0]
    cos_t, sin_t, segb, before, after, validb, rows, inside = tables
    line.did(rows, inside)
    norms_o = line.after(norms_o)
    first, second = jnp.where(first_x, norms, norms_o), jnp.where(first_x, norms_o, norms)
    gains = jnp.concatenate([first[:7], second[:7]], axis=1).astype(F32)
    kern = jnp.concatenate(
        [first[8:].reshape(KER // 2, D), second[8:].reshape(KER // 2, D)], axis=0
    ).astype(F32)
    g_first, g_attend, g_conv, g_bn, b_bn, g_second, g_final = (gains[i : i + 1] for i in range(7))
    line.did(gains)
    pass_on("up1", "down1")

    tall = MB * slots
    tm = 256
    x_flat = frames.reshape(tall, D)

    def row_spec(width):
        return pl.BlockSpec((tm, width), lambda i: (i, 0))

    x1, a1, h1, g1 = pl.pallas_call(
        feed_kernel,
        name="feed",
        grid=(tall // tm,),
        in_specs=[SMEM, row_spec(D), full((1, D)), *[ANY] * 6],
        out_specs=[row_spec(D), row_spec(D), row_spec(FF), row_spec(FF)],
        out_shape=[out((tall, D), F32), out((tall, D), BF16)] + [out((tall, FF), BF16)] * 2,
        scratch_shapes=weight_scratch((D, FF), (FF, D)),
        cost_estimate=cost(4 * tall * D * FF, 2e7),
    )(line.after(where), x_flat, g_first, *whole("up1"), *whole("down1"))
    line.did(a1)
    pass_on("joint", "aout")

    def cut(array):
        return array.reshape(MB, slots, array.shape[-1])

    def by_micro(*shape):
        rest = (0,) * len(shape)
        return pl.BlockSpec((1,) + shape, lambda i: (i,) + rest)

    x1 = cut(x1)
    x2, a2, qh, kh, vh, probs, mixed = pl.pallas_call(
        attend_kernel,
        name="attend",
        grid=(MB,),
        in_specs=[
            SMEM, by_micro(slots, D), full((1, D)), by_micro(slots, 128), by_micro(slots, 128),
            by_micro(slots, 128), by_micro(2, slots), *[ANY] * 6,
        ],
        out_specs=[by_micro(slots, D)] * 5 + [by_micro(HEADS, slots, slots), by_micro(slots, D)],
        out_shape=[out((MB, slots, D), F32)] + [out((MB, slots, D), BF16)] * 4
        + [out((MB, HEADS, slots, slots), BF16), out((MB, slots, D), BF16)],
        scratch_shapes=[
            pltpu.VMEM((D, 3 * D), BF16), pltpu.VMEM((D, D), BF16), pltpu.VMEM((slots, slots), F32),
            pltpu.SemaphoreType.DMA((6,)),
        ],
        cost_estimate=cost(MB * slots * (8 * D * D + 8 * slots * D), 3e7),
    )(line.after(where), x1, g_attend, cos_t, sin_t, segb, rows, *whole("joint"), *whole("aout"))
    line.did(a2)
    pass_on("cin")

    pad_rows = slots + 40

    tables_spec = [by_micro(slots, 128)] * 3
    a3, glu, p1, p2, conv, stats = pl.pallas_call(
        conv_kernel,
        name="conv",
        grid=(MB,),
        in_specs=[
            SMEM, SMEM, by_micro(slots, D), full((1, D)), full((KER, D)), *tables_spec, *[ANY] * 3,
        ],
        out_specs=[by_micro(slots, D)] * 5 + [by_micro(4, D)],
        out_shape=[
            out((MB, slots, D), BF16), out((MB, slots, D), F32), out((MB, slots, D), BF16),
            out((MB, slots, D), BF16), out((MB, slots, D), F32), out((MB, 4, D), F32),
        ],
        scratch_shapes=[
            pltpu.VMEM((D, 2 * D), BF16), pltpu.VMEM((pad_rows, D), F32),
            pltpu.VMEM((8, pad_rows - 8, D), F32), pltpu.SemaphoreType.DMA((3,)),
        ],
        cost_estimate=cost(MB * (4 * slots * D * D + 60 * KER * slots * D), 2e7),
    )(line.after(where), inside, x2, g_conv, kern, validb, before, after, *whole("cin"))
    stats = stats.reshape(4 * MB, D)
    line.did(stats)
    pass_on("cout", "up2", "down2")
    sync = Sum(line, sizes, stats)
    while sync.step():
        pass
    total = sync.value.reshape(MB, 4, D)
    mid_gains = jnp.concatenate([g_bn, b_bn, g_second, g_final], axis=0)
    tiles = slots // tm

    def tile_spec(width):
        return pl.BlockSpec((tm, width), lambda m, i: (m * tiles + i, 0))

    def per_micro(rows_of):
        return pl.BlockSpec((1, rows_of, D), lambda m, *_: (m, 0, 0))

    enc, a4, e3, a5, h2, dz2, e4, db, dx3, mid_sums = pl.pallas_call(
        middle_kernel,
        name="middle",
        grid=(MB, tiles),
        in_specs=[SMEM, per_micro(4), full((4, D)), *[tile_spec(D)] * 3, *[ANY] * 9],
        out_specs=[tile_spec(D)] * 4 + [tile_spec(FF)] * 2 + [tile_spec(D)] * 3 + [per_micro(8)],
        out_shape=[out((tall, D), BF16)] * 4 + [out((tall, FF), BF16)] * 2
        + [out((tall, D), BF16)] + [out((tall, D), F32)] * 2 + [out((MB, 8, D), F32)],
        scratch_shapes=[
            pltpu.VMEM((D, D), BF16), pltpu.VMEM((D, FF), BF16), pltpu.VMEM((FF, D), BF16),
            pltpu.VMEM((tm, FF), BF16), pltpu.SemaphoreType.DMA((9,)),
        ],
        cost_estimate=cost(tall * (8 * D * FF + 4 * D * D), 4e7),
    )(line.after(where), total, mid_gains, conv.reshape(tall, D), x2.reshape(tall, D),
      output_grad.reshape(tall, D), *whole("cout"), *whole("up2"), *whole("down2"))
    stats = mid_sums[:, :2].reshape(2 * MB, D)
    line.did(stats)
    sync = Sum(line, sizes, stats)

    def product(*sides):
        found = []
        for side in sides:
            if isinstance(side, list):
                found.append([(array, 0) for array in side])
            else:
                found.append([(side.reshape(tall, side.shape[-1]), m) for m in range(MB)])
        return found

    def weights(name, *products):
        send = weight_call(name + "_send", products, line.after(1 - core), line, slots)
        got = swap(send, "dp", 1, sizes["dp"])
        if name == "weights_up":
            chain_d.step()
        return got, weight_call(name + "_keep", products, line.after(core), line, slots)

    pair = weights("weights_second", product(h2, e4), product(a5, dz2), product(a4, e3))
    chain_a = Background(line, sizes, ((FF, D), (D, FF), (D, D)), *pair)
    while sync.step():
        pass
    chain_a.step()
    back = sync.value.reshape(MB, 2, D)
    back_gains = jnp.concatenate([g_bn, g_conv], axis=0)
    dg, dx2, e2, kern_sum, sums_conv = pl.pallas_call(
        conv_back_kernel,
        name="conv_back",
        grid=(MB,),
        in_specs=[
            SMEM, SMEM, per_micro(4), per_micro(2), full((2, D)), full((KER, D)),
            *[by_micro(slots, D)] * 7, *tables_spec, *[ANY] * 3,
        ],
        out_specs=[
            by_micro(slots, 2 * D), by_micro(slots, D), by_micro(slots, D), full((KER, D)), per_micro(8),
        ],
        out_shape=[
            out((MB, slots, 2 * D), BF16), out((MB, slots, D), F32), out((MB, slots, D), BF16),
            out((KER, D), F32), out((MB, 8, D), F32),
        ],
        scratch_shapes=[
            pltpu.VMEM((D, 2 * D), BF16), pltpu.VMEM((pad_rows, D), F32),
            pltpu.VMEM((8, pad_rows - 8, D), F32), pltpu.VMEM((slots, D), F32),
            pltpu.VMEM((KER, 8, D), F32), pltpu.SemaphoreType.DMA((3,)),
        ],
        cost_estimate=cost(MB * (4 * slots * D * D + 120 * KER * slots * D), 3e7),
    )(line.after(where), inside, total, back, back_gains, kern, conv, cut(db), glu, p1, p2, x2, cut(dx3),
      validb, before, after, *whole("cin"))
    line.did(sums_conv)
    pair = weights("weights_conv", product(a3, dg), product(mixed, e2))
    chain_c = Background(line, sizes, ((D, 2 * D), (D, D)), *pair)
    chain_a.step()
    chain_c.step()

    dj, dx1, e1, sums_attend = pl.pallas_call(
        attend_back_kernel,
        name="attend_back",
        grid=(MB,),
        in_specs=[
            SMEM, by_micro(slots, D), full((1, D)), *[by_micro(slots, 128)] * 2,
            *[by_micro(slots, D)] * 4, by_micro(HEADS, slots, slots), *[ANY] * 6,
        ],
        out_specs=[by_micro(slots, 3 * D), by_micro(slots, D), by_micro(slots, D), by_micro(8, D)],
        out_shape=[
            out((MB, slots, 3 * D), BF16), out((MB, slots, D), F32), out((MB, slots, D), BF16),
            out((MB, 8, D), F32),
        ],
        scratch_shapes=[
            pltpu.VMEM((D, 3 * D), BF16), pltpu.VMEM((D, D), BF16), pltpu.VMEM((slots, D), BF16),
            pltpu.VMEM((slots, D), F32), pltpu.VMEM((slots, D), F32), pltpu.SemaphoreType.DMA((6,)),
        ],
        cost_estimate=cost(MB * slots * (8 * D * D + 16 * slots * D), 3e7),
    )(line.after(where), x1, g_attend, cos_t, sin_t, dx2, qh, kh, vh, probs,
      *whole("joint"), *whole("aout"))
    line.did(sums_attend)
    chain_c.step()
    reduce_behind((chain_a, chain_c), sizes["dp"])
    pair = weights("weights_down", product(h1, e1), product(a2, dj))
    chain_d = Chain(line, sizes, ((FF, D), (D, 3 * D)), *pair, 3)
    dx1, e1 = dx1.reshape(tall, D), e1.reshape(tall, D)

    def back_feed(m):
        def at_micro(width):
            return pl.BlockSpec((tm, width), lambda i: (m * tiles + i, 0))

        found = pl.pallas_call(
            feed_back_kernel,
            name=f"feed_back_{m}",
            grid=(tiles,),
            in_specs=[
                SMEM, at_micro(D), full((1, D)), at_micro(D), at_micro(D), at_micro(FF), *[ANY] * 6,
            ],
            out_specs=[row_spec(D), row_spec(FF), full((8, D))],
            out_shape=[out((slots, D), BF16), out((slots, FF), BF16), out((8, D), F32)],
            scratch_shapes=weight_scratch((D, FF), (FF, D)),
            cost_estimate=cost(4 * slots * D * FF, 1e7),
        )(line.after(where), x_flat, g_first, dx1, e1, g1, *whole("up1"), *whole("down1"))
        line.did(found[2])
        return found

    chain_d.step()
    feed_backs = [back_feed(0)]
    feed_backs.append(back_feed(1))
    pair = weights("weights_up", product(a1, [f[1] for f in feed_backs]))
    chain_f = Chain(line, sizes, ((D, FF),), *pair, 3)

    mid_sums = mid_sums[0] + mid_sums[1]
    small = jnp.concatenate(
        [
            kern_sum,
            feed_backs[0][2][0:1] + feed_backs[1][2][0:1],
            sums_attend[0, 0:1] + sums_attend[1, 0:1],
            sums_conv[0, 0:1] + sums_conv[1, 0:1],
            mid_sums[1:2],
            mid_sums[0:1],
            mid_sums[2:4],
            jnp.zeros((1, D), F32),
        ],
        axis=0,
    )
    line.did(small)
    small = Sum(line, sizes, small, (2,))
    chain_f.step()
    chain_d.step()
    small.step()
    chain_d.step()
    small.step()
    chain_d.step()
    chain_f.step()
    small.step()
    chain_d.step()
    small.step()
    chain_f.step()
    chain_d.step()
    chain_f.step()
    chain_a.pass_on()
    chain_f.step()
    chain_d.step()
    small.step()
    chain_f.step()
    chain_a.step()
    chain_c.pass_on()
    chain_f.step()
    chain_d.step()
    chain_c.step()
    chain_f.step()
    chain_f.step()
    for chain in (chain_d, chain_f):
        while chain.plan:
            chain.step()
    while small.plan:
        small.step()
    small = small.value
    kern_grad = lax.dynamic_slice_in_dim(small, x_at[0] * (KER // 2), KER // 2, axis=0)
    vectors = lax.dynamic_slice_in_dim(small[KER:], x_at[0] * (D // 2), D // 2, axis=1)
    down2_g, up2_g, cout_g = chain_a.result
    cin_g, aout_g = chain_c.result
    down1_g, joint_g = chain_d.result
    (up1_g,) = chain_f.result
    fgrad = jnp.stack([f[0] for f in feed_backs])
    return (
        enc.reshape(MB, slots, D), fgrad, vectors[0], up1_g, down1_g, vectors[1], joint_g, aout_g,
        vectors[2], cin_g, kern_grad, vectors[3], vectors[4], cout_g, vectors[5], up2_g, down2_g,
        vectors[6],
    )


def solution(mesh):
    split = P(None, ("dp", "fsdp"), None)
    row, mat = P("fsdp"), P("fsdp", None)
    weights = (row, mat, mat, row, mat, mat, row, mat, mat, row, row, mat, row, mat, mat, row)
    return jax.shard_map(
        functools.partial(body, dict(mesh.shape)),
        mesh=mesh,
        in_specs=(split, split, P(None, ("dp", "fsdp"))) + weights + (split,),
        out_specs=(split, split) + weights,
        check_vma=False,
    )
```

```python
import functools
import math

import jax
import jax.numpy as jnp
from jax import lax
from jax.experimental import pallas as pl
from jax.experimental.pallas import tpu as pltpu
from jax.sharding import PartitionSpec as P

HEADS = 8
KER = 32
HDIM = 64
MB = 2
D = 512
FF = 2048
EPS = 1e-05
PAD = 16
CHUNK = 32
F32 = jnp.float32
BF16 = jnp.bfloat16
ANY = pl.BlockSpec(memory_space=pl.ANY)
SMEM = pl.BlockSpec(memory_space=pltpu.SMEM)
VMEM = pl.BlockSpec(memory_space=pltpu.VMEM)


def swap(value, axis, bit, size):
    return lax.ppermute(value, axis, [(i, i ^ bit) for i in range(size)])


def bits_of(size):
    return [1 << i for i in range(size.bit_length() - 1)]


class Line:
    def __init__(self):
        self.last = ()

    def after(self, value):
        return lax.optimization_barrier((value, self.last))[0] if self.last else value

    def did(self, *values):
        self.last = values


def add_split(keep, got, index):
    parts = []
    for at in (index, 1 - index):
        left = lax.dynamic_index_in_dim(keep, at, 0, keepdims=False)
        right = lax.dynamic_index_in_dim(got, at, 0, keepdims=False)
        parts.append((left.astype(F32) + right.astype(F32)).astype(BF16))
    return parts


def unpack_kernel(shapes, index, keep, got, *outs):
    at = 0
    for (m, n), target in zip(shapes, outs):
        quarter = m // 4
        for source, core in ((keep, index[0]), (got, 1 - index[0])):
            rows = pl.ds(pl.multiple_of(core * quarter, quarter), quarter)
            for j in range(n // 512):
                first = at + j * quarter
                target[rows, j * 512 : (j + 1) * 512] = source[first : first + quarter].astype(F32)
        at += (n // 512) * quarter


class Chain:
    def __init__(self, line, sizes, shapes, got, keep, halved):
        self.line, self.sizes, self.shapes, self.keep = line, sizes, shapes, keep
        bits = bits_of(sizes["dp"])[1:]
        halved = bits[:halved]
        whole = bits[len(halved) :]
        self.plan = [("split", "x")] + [("split", bit) for bit in halved] + [("add", bit) for bit in whole]
        self.plan += [("last", None)] + [("join", bit) for bit in halved[::-1]] + [("unpack", 1)]
        self.order = ["x"] + halved + whole + halved[::-1] + [1]
        self.got = got
        self.result = None

    def where(self, bit):
        if bit == "x":
            return lax.axis_index("fsdp").astype(jnp.int32)
        return ((lax.axis_index("dp") & bit) > 0).astype(jnp.int32)

    def send(self, value):
        bit = self.order.pop(0)
        if bit == "x":
            self.got = swap(value, "fsdp", 1, 2)
        else:
            self.got = swap(value, "dp", bit, self.sizes["dp"])

    def step(self):
        kind, bit = self.plan.pop(0)
        got = self.line.after(self.got)
        keep = self.keep
        if kind == "split":
            rows = keep.size // (2 * D)
            self.keep, send = add_split(keep.reshape(2, rows, D), got.reshape(2, rows, D), self.where(bit))
            self.line.did(send, self.keep)
            self.send(send)
        elif kind in ("add", "last"):
            self.keep = (keep.astype(F32) + got.astype(F32)).astype(BF16)
            self.line.did(self.keep)
            self.send(self.keep)
        elif kind == "join":
            low = self.where(bit) == 0
            self.keep = jnp.concatenate([jnp.where(low, keep, got), jnp.where(low, got, keep)], axis=0)
            self.line.did(self.keep)
            self.send(self.keep)
        else:
            outs = [out((m // 2, n), F32) for m, n in self.shapes]
            self.result = pl.pallas_call(
                functools.partial(unpack_kernel, self.shapes),
                name="unpack",
                in_specs=[SMEM, VMEM, VMEM],
                out_specs=[VMEM] * len(outs),
                out_shape=outs,
                cost_estimate=cost(0, 12 * keep.size),
            )(self.where(1).reshape(1), keep, got)
            self.line.did(self.result[-1])


class Background(Chain):
    def __init__(self, line, sizes, shapes, got, keep):
        super().__init__(line, sizes, shapes, got, keep, 0)
        self.plan = [("split", "x"), ("total", None), ("unpack", 1)]

    def step(self):
        if self.plan[0][0] != "total":
            return super().step()
        self.plan.pop(0)
        got = self.line.after(self.got)
        self.keep = (self.keep.astype(F32) + got.astype(F32)).astype(BF16)
        self.line.did(self.keep)

    def pass_on(self):
        self.keep = self.line.after(self.keep)
        self.got = swap(self.keep, "dp", 1, self.sizes["dp"])


def reduce_behind(chains, size):
    groups = [[i for i in range(size) if i % 2 == c] for c in range(2)]
    totals = lax.psum(tuple(c.keep for c in chains), "dp", axis_index_groups=groups)
    for chain, total in zip(chains, totals):
        chain.keep = total


class Sum:
    def __init__(self, line, sizes, value, late=()):
        self.line, self.sizes, self.value = line, sizes, value
        bits = bits_of(sizes["dp"])
        self.plan = [bit for bit in bits if bit not in late] + list(late) + ["x"]
        self.start()

    def start(self):
        bit = self.plan.pop(0)
        if bit == "x":
            self.got = swap(self.value, "fsdp", 1, 2)
        else:
            self.got = swap(self.value, "dp", bit, self.sizes["dp"])

    def step(self):
        self.value = self.value + self.line.after(self.got)
        self.line.did(self.value)
        if self.plan:
            self.start()
            return True
        return False


def dot(left, right):
    return lax.dot_general(left, right, (((1,), (0,)), ((), ())), preferred_element_type=F32)


def dot_nt(left, right):
    return lax.dot_general(left, right, (((1,), (1,)), ((), ())), preferred_element_type=F32)


def dot_tn(left, right):
    return lax.dot_general(left, right, (((0,), (0,)), ((), ())), preferred_element_type=F32)


def sigmoid(values):
    return 0.5 * jnp.tanh(0.5 * values) + 0.5


def norm(values):
    centered = values - jnp.mean(values, axis=-1, keepdims=True)
    inverse = lax.rsqrt(jnp.mean(centered * centered, axis=-1, keepdims=True) + EPS)
    return centered * inverse, inverse


def norm_back(grad, rows, inverse, gain):
    scaled = grad * gain
    return inverse * (
        scaled
        - jnp.mean(scaled, axis=-1, keepdims=True)
        - rows * jnp.mean(scaled * rows, axis=-1, keepdims=True)
    )


def column_sum(values):
    return jnp.sum(values, axis=0, keepdims=True)


def fetch(where, sources, targets, sem):
    copies = []
    for i, (mine, near, far, *column) in enumerate(sources):
        rows = mine.shape[0]
        piece = rows // 2
        start = (1 - where[0]) * rows
        places = (where[0] * rows, start + where[1] * piece, start + (1 - where[1]) * piece)
        for j, source in enumerate((mine, near, far)):
            at = pl.multiple_of(places[j], piece)
            if j and column:
                source = source.at[:, pl.ds(column[0], mine.shape[1])]
            copies.append(
                pltpu.make_async_copy(
                    source, targets[i].at[pl.ds(at, source.shape[0])], sem.at[3 * i + j]
                )
            )
    for copy in copies:
        copy.start()
    for copy in copies:
        copy.wait()


def weight_scratch(*shapes):
    return [pltpu.VMEM(shape, BF16) for shape in shapes] + [
        pltpu.SemaphoreType.DMA((3 * len(shapes),))
    ]


def tile4(values):
    return jnp.concatenate([values] * 4, axis=1)


def turn(values, cosine, sine):
    lane = lax.broadcasted_iota(jnp.int32, (values.shape[0], 128), 1)
    first = (lane & 63) < 32
    parts = []
    for c in range(4):
        u = values[:, c * 128 : (c + 1) * 128]
        swapped = jnp.where(first, pltpu.roll(u, 96, 1), pltpu.roll(u, 32, 1))
        parts.append(u * cosine + swapped * sine)
    return jnp.concatenate(parts, axis=1)


def head_masks():
    lane = lax.broadcasted_iota(jnp.int32, (1, 128), 1)
    return [((lane >> 6) == e).astype(F32).astype(BF16) for e in range(2)]


def feed_kernel(idx, x, gain, um, un, uf, dm, dn, df, x1, a1, h1, g1, u, d, sem):
    @pl.when(pl.program_id(0) == 0)
    def _():
        fetch(idx, ((um, un, uf), (dm, dn, df)), (u, d), sem)

    v = x[...].astype(F32)
    a = (norm(v)[0] * gain[...]).astype(BF16)
    a1[...] = a
    acc = None
    for j in range(4):
        c = slice(j * 512, (j + 1) * 512)
        z = dot(a, u[:, c])
        s = sigmoid(z)
        h = z * s
        g1[:, c] = (s + h * (1.0 - s)).astype(BF16)
        h = h.astype(BF16)
        h1[:, c] = h
        part = dot(h, d[c, :])
        acc = part if acc is None else acc + part
    x1[...] = v + 0.5 * acc


def attend_kernel(
    idx, x1, gain, cos, sin, segb, rows, jm, jn, jf, om, on, of,
    x2, a2, qo, ko, vo, pr, mixed, wj, wo, bias, sem,
):
    @pl.when(pl.program_id(0) == 0)
    def _():
        fetch(idx, ((jm, jn, jf, 0), (om, on, of, 3 * D)), (wj, wo), sem)

    v = x1[0]
    a = (norm(v)[0] * gain[...]).astype(BF16)
    a2[0] = a
    cosine, sine = cos[0], sin[0]
    qo[0] = (turn(dot(a, wj[:, :512]), cosine, sine) * HDIM ** (-0.5)).astype(BF16)
    ko[0] = turn(dot(a, wj[:, 512:1024]), cosine, sine).astype(BF16)
    vo[0] = dot(a, wj[:, 1024:]).astype(BF16)
    size = bias.shape[0]
    row = lax.broadcasted_iota(jnp.int32, (size, size), 0)
    col = lax.broadcasted_iota(jnp.int32, (size, size), 1)
    allowed = (tile4(segb[0]) == rows[0, 0:1, :]) & ((rows[0, 1:2, :] > 0) | (row == col))
    bias[...] = jnp.where(allowed, 0.0, -1000000000.0)
    masks = head_masks()

    def pair(p, carry):
        c = pl.ds(pl.multiple_of(p * 128, 128), 128)
        q, k, val = qo[0, :, c], ko[0, :, c], vo[0, :, c]
        total = None
        for e in range(2):
            s = dot_nt(q * masks[e], k) + bias[...]
            ex = jnp.exp(s - jnp.max(s, axis=-1, keepdims=True))
            prob = (ex * (1.0 / jnp.sum(ex, axis=-1, keepdims=True))).astype(BF16)
            pr[0, 2 * p + e] = prob
            part = dot(prob, val * masks[e])
            total = part if total is None else total + part
        mixed[0, :, c] = total.astype(BF16)
        return carry

    lax.fori_loop(0, HEADS // 2, pair, 0)
    x2[0] = v + dot(mixed[0], wo[...])


def conv_taps(padded, shifts):
    rows = shifts.shape[1]
    for b in range(8):
        shifts[b] = padded[b : b + rows, :]


def conv_kernel(
    idx, inside, x2, gain, kern, validb, before, after, wm, wn, wf,
    a3, glu, p1, p2, cout, stats, w, padded, shifts, sem,
):
    micro = pl.program_id(0)
    size = x2.shape[1]

    @pl.when(micro == 0)
    def _():
        fetch(idx, ((wm, wn, wf, 0),), (w,), sem)
        padded[0:PAD] = jnp.zeros((PAD, D), F32)
        padded[PAD + size :] = jnp.zeros((padded.shape[0] - PAD - size, D), F32)

    a = (norm(x2[0])[0] * gain[...]).astype(BF16)
    a3[0] = a
    valid = tile4(validb[0])
    g1 = dot(a, w[:, :512])
    s = sigmoid(dot(a, w[:, 512:])) * valid
    g = g1 * s
    glu[0] = g
    p1[0] = s.astype(BF16)
    p2[0] = (g * (1.0 - s)).astype(BF16)
    padded[PAD : PAD + size] = g
    conv_taps(padded, shifts)

    def step(i, carry):
        r0 = pl.multiple_of(i * CHUNK, CHUNK)

        def run(masked):
            if masked:
                low, high = before[0, pl.ds(r0, CHUNK), :], after[0, pl.ds(r0, CHUNK), :]
            acc = [jnp.zeros((CHUNK, 128), F32) for _ in range(4)]
            for o in range(KER):
                shift_by = o - (KER - 1) // 2
                a8, b = divmod(shift_by + PAD, 8)
                if masked and shift_by < 0:
                    keep = low >= float(-shift_by)
                elif masked and shift_by > 0:
                    keep = high >= float(shift_by)
                for c in range(4):
                    cs = slice(c * 128, (c + 1) * 128)
                    value = shifts[b, pl.ds(r0 + 8 * a8, CHUNK), cs]
                    if masked and shift_by != 0:
                        value = jnp.where(keep, value, 0.0)
                    acc[c] = acc[c] + kern[o : o + 1, cs] * value
            for c in range(4):
                cout[0, pl.ds(r0, CHUNK), c * 128 : (c + 1) * 128] = acc[c]

        flag = inside[micro, i]
        pl.when(flag > 0)(functools.partial(run, False))
        pl.when(flag == 0)(functools.partial(run, True))
        return carry

    lax.fori_loop(0, size // CHUNK, step, 0)
    result = cout[0]
    weighted = result * valid
    stats[0, 0:1] = column_sum(weighted)
    stats[0, 1:2] = column_sum(weighted * result)
    stats[0, 2:3] = column_sum(valid)
    stats[0, 3:4] = jnp.zeros((1, D), F32)


def middle_kernel(
    idx, total, gains, conv, x2, og, cm, cn, cf, um, un, uf, dm, dn, df,
    enc, a4, e3, a5, h2, dz, e4, db, dx3, sums, wc, u, d, deriv, sem,
):
    @pl.when((pl.program_id(0) == 0) & (pl.program_id(1) == 0))
    def _():
        fetch(idx, ((cm, cn, cf, 2 * D), (um, un, uf), (dm, dn, df)), (wc, u, d), sem)

    @pl.when(pl.program_id(1) == 0)
    def _():
        sums[...] = jnp.zeros(sums.shape, F32)

    gain_b, bias_b, gain_2, gain_f = (gains[i : i + 1] for i in range(4))
    count = total[0, 2:3]
    mean = total[0, 0:1] / count
    inverse = lax.rsqrt(total[0, 1:2] / count - mean * mean + EPS)
    unit = (conv[...] - mean) * inverse
    act = unit * gain_b + bias_b
    s_act = sigmoid(act)
    a = (act * s_act).astype(BF16)
    a4[...] = a
    v3 = x2[...] + dot(a, wc[...])
    n5, inv5 = norm(v3)
    a = (n5 * gain_2).astype(BF16)
    a5[...] = a
    acc = None
    for j in range(4):
        c = slice(j * 512, (j + 1) * 512)
        z = dot(a, u[:, c])
        s = sigmoid(z)
        h = z * s
        deriv[:, c] = (s + h * (1.0 - s)).astype(BF16)
        h = h.astype(BF16)
        h2[:, c] = h
        part = dot(h, d[c, :])
        acc = part if acc is None else acc + part
    n6, inv6 = norm(v3 + 0.5 * acc)
    enc[...] = (n6 * gain_f).astype(BF16)
    dy = og[...].astype(F32)
    sums[0, 3:4] += column_sum(dy * n6)
    grad4 = norm_back(dy, n6, inv6, gain_f)
    e = (0.5 * grad4).astype(BF16)
    e4[...] = e
    acc = None
    for j in range(4):
        c = slice(j * 512, (j + 1) * 512)
        g = (dot_nt(e, d[c, :]) * deriv[:, c].astype(F32)).astype(BF16)
        dz[:, c] = g
        part = dot_nt(g, u[:, c])
        acc = part if acc is None else acc + part
    sums[0, 2:3] += column_sum(acc * n5)
    grad3 = grad4 + norm_back(acc, n5, inv5, gain_2)
    dx3[...] = grad3
    e = grad3.astype(BF16)
    e3[...] = e
    dact = dot_nt(e, wc[...]) * (s_act * (1.0 + act * (1.0 - s_act)))
    db[...] = dact
    sums[0, 0:1] += column_sum(dact)
    sums[0, 1:2] += column_sum(dact * unit)


def conv_back_kernel(
    idx, inside, total, back, gains, kern, conv, db, glu, p1, p2, x2, dx3, validb, before, after, wm, wn, wf,
    dg, dx2, e2, dk, sums, w, padded, shifts, dglu, dkacc, sem,
):
    micro = pl.program_id(0)
    size = x2.shape[1]

    @pl.when(micro == 0)
    def _():
        fetch(idx, ((wm, wn, wf, 0),), (w,), sem)
        padded[0:PAD] = jnp.zeros((PAD, D), F32)
        padded[PAD + size :] = jnp.zeros((padded.shape[0] - PAD - size, D), F32)
        dkacc[...] = jnp.zeros(dkacc.shape, F32)

    gain_b, gain_c = gains[0:1], gains[1:2]
    count = total[0, 2:3]
    mean = total[0, 0:1] / count
    inverse = lax.rsqrt(total[0, 1:2] / count - mean * mean + EPS)
    share = inverse / count
    at_one, at_unit = share * (gain_b * back[0, 0:1]), share * (gain_b * back[0, 1:2])
    unit = (conv[0] - mean) * inverse
    padded[PAD : PAD + size] = db[0] * (inverse * gain_b) - tile4(validb[0]) * (at_one + unit * at_unit)
    conv_taps(padded, shifts)

    def step(i, carry):
        r0 = pl.multiple_of(i * CHUNK, CHUNK)

        def run(masked):
            if masked:
                low, high = before[0, pl.ds(r0, CHUNK), :], after[0, pl.ds(r0, CHUNK), :]
            for c in range(4):
                cs = slice(c * 128, (c + 1) * 128)
                own = glu[0, pl.ds(r0, CHUNK), cs]
                acc = jnp.zeros((CHUNK, 128), F32)
                for o in range(KER):
                    shift_by = (KER - 1) // 2 - o
                    a8, b = divmod(shift_by + PAD, 8)
                    value = shifts[b, pl.ds(r0 + 8 * a8, CHUNK), cs]
                    if masked and shift_by < 0:
                        value = jnp.where(low >= float(-shift_by), value, 0.0)
                    elif masked and shift_by > 0:
                        value = jnp.where(high >= float(shift_by), value, 0.0)
                    acc = acc + kern[o : o + 1, cs] * value
                    prod = own * value
                    part = prod[0:8]
                    for q in range(1, CHUNK // 8):
                        part = part + prod[8 * q : 8 * q + 8]
                    dkacc[o, :, cs] += part
                dglu[pl.ds(r0, CHUNK), cs] = acc

        flag = inside[micro, i]
        pl.when(flag > 0)(functools.partial(run, False))
        pl.when(flag == 0)(functools.partial(run, True))
        return carry

    lax.fori_loop(0, size // CHUNK, step, 0)
    dk[...] = jnp.sum(dkacc[...], axis=1)
    grad = dglu[...]
    g1 = (grad * p1[0].astype(F32)).astype(BF16)
    g2 = (grad * p2[0].astype(F32)).astype(BF16)
    dg[0, :, :512] = g1
    dg[0, :, 512:] = g2
    da = dot_nt(g1, w[:, :512]) + dot_nt(g2, w[:, 512:])
    n3, inv3 = norm(x2[0])
    sums[0, 0:1] = column_sum(da * n3)
    sums[0, 1:8] = jnp.zeros((7, D), F32)
    result = dx3[0] + norm_back(da, n3, inv3, gain_c)
    dx2[0] = result
    e2[0] = result.astype(BF16)


def attend_back_kernel(
    idx, x1, gain, cos, sin, dx2, q, k, v, pr, jm, jn, jf, om, on, of,
    dj, dx1, e1, sums, wj, wo, dmix, dq, dkey, sem,
):
    @pl.when(pl.program_id(0) == 0)
    def _():
        fetch(idx, ((jm, jn, jf, 0), (om, on, of, 3 * D)), (wj, wo), sem)

    grad2 = dx2[0]
    dmix[...] = dot_nt(grad2.astype(BF16), wo[...]).astype(BF16)
    masks = head_masks()

    def pair(p, carry):
        c = pl.ds(pl.multiple_of(p * 128, 128), 128)
        qp, kp, vp, gp = q[0, :, c], k[0, :, c], v[0, :, c], dmix[:, c]
        parts = [None, None, None]
        for e in range(2):
            prob = pr[0, 2 * p + e]
            grad = gp * masks[e]
            dp = dot_nt(grad, vp)
            wide = prob.astype(F32)
            prod = wide * dp
            ds = (prod - wide * jnp.sum(prod, axis=-1, keepdims=True)).astype(BF16)
            new = (dot(ds, kp * masks[e]), dot_tn(ds, qp * masks[e]), dot_tn(prob, grad))
            parts = [b if a is None else a + b for a, b in zip(parts, new)]
        dq[:, c] = parts[0]
        dkey[:, c] = parts[1]
        dj[0, :, pl.ds(pl.multiple_of(1024 + p * 128, 128), 128)] = parts[2].astype(BF16)
        return carry

    lax.fori_loop(0, HEADS // 2, pair, 0)
    cosine, sine = cos[0], -sin[0]
    dj[0, :, :512] = turn(dq[...] * HDIM ** (-0.5), cosine, sine).astype(BF16)
    dj[0, :, 512:1024] = turn(dkey[...], cosine, sine).astype(BF16)
    da = dot_nt(dj[0], wj[...])
    n2, inv2 = norm(x1[0])
    sums[0, 0:1] = column_sum(da * n2)
    sums[0, 1:8] = jnp.zeros((7, D), F32)
    out = grad2 + norm_back(da, n2, inv2, gain[...])
    dx1[0] = out
    e1[0] = (0.5 * out).astype(BF16)


def feed_back_kernel(idx, x, gain, dx1, e1, g1, um, un, uf, dm, dn, df, fg, dz, sums, u, d, sem):
    @pl.when(pl.program_id(0) == 0)
    def _():
        fetch(idx, ((um, un, uf), (dm, dn, df)), (u, d), sem)
        sums[...] = jnp.zeros(sums.shape, F32)

    e = e1[...]
    acc = None
    for j in range(4):
        c = slice(j * 512, (j + 1) * 512)
        g = (dot_nt(e, d[c, :]) * g1[:, c].astype(F32)).astype(BF16)
        dz[:, c] = g
        part = dot_nt(g, u[:, c])
        acc = part if acc is None else acc + part
    n1, inv1 = norm(x[...].astype(F32))
    sums[0:1] += column_sum(acc * n1)
    fg[...] = (dx1[...] + norm_back(acc, n1, inv1, gain[...])).astype(BF16)


def weight_kernel(plan, core, *refs):
    ins, result = refs[:-1], refs[-1]
    at = 0
    for i, blocks in enumerate(plan):
        l0, r0, l1, r1 = ins[4 * i : 4 * i + 4]
        rows = l0.shape[1]
        for j in range(blocks):
            c = slice(j * 512, (j + 1) * 512)
            result[0, at : at + rows] = (
                dot_tn(l0[...], r0[:, c]) + dot_tn(l1[...], r1[:, c])
            ).astype(BF16)
            at += rows


def full(shape):
    zeros = (0,) * len(shape)
    return pl.BlockSpec(shape, lambda *_: zeros)


def out(shape, dtype):
    return jax.ShapeDtypeStruct(shape, dtype)


def cost(flops, nbytes):
    return pl.CostEstimate(flops=int(flops), bytes_accessed=int(nbytes), transcendentals=0)


def micro_spec(shape, micro):
    rest = (0,) * len(shape)
    return pl.BlockSpec((1,) + shape, lambda *_: (micro,) + rest)


def weight_call(name, products, core, line, slots_of):
    plan, specs, arrays, rows, flops = [], [], [], 0, 0

    def quarter(step, core_ref):
        return step * 2 + core_ref[0]

    for lefts, rights in products:
        (l0, _), (r0, _) = lefts[0], rights[0]
        slots = slots_of
        m, n = l0.shape[1], r0.shape[1]
        plan.append(n // 512)
        rows += (n // 512) * (m // 4)
        flops += 2 * slots * m * n
        for (left, i), (right, j) in zip(lefts, rights):
            specs.append(pl.BlockSpec((slots, m // 4), lambda s, ref, i=i: (i, quarter(s, ref))))
            specs.append(pl.BlockSpec((slots, n), lambda s, ref, j=j: (j, 0)))
            arrays += [left, right]
    nbytes = sum(a.size * 2 for a in arrays) + rows * 512 * 8
    found = pl.pallas_call(
        functools.partial(weight_kernel, tuple(plan)),
        name=name,
        grid_spec=pltpu.PrefetchScalarGridSpec(
            num_scalar_prefetch=1,
            grid=(2,),
            in_specs=specs,
            out_specs=pl.BlockSpec((1, rows, D), lambda s, ref: (s, 0, 0)),
        ),
        out_shape=out((2, rows, D), BF16),
        cost_estimate=cost(flops, nbytes),
    )(core, *arrays)
    line.did(found)
    return found


def layout(lengths, mask, slots):
    ends = jnp.cumsum(lengths, axis=1)
    starts = ends - lengths
    slot = jnp.arange(slots, dtype=jnp.int32)
    reached = slot[None, :, None] >= ends[:, None, :]
    segment = jnp.sum(reached.astype(jnp.int32), axis=2)
    member = segment[:, :, None] == jnp.arange(lengths.shape[1], dtype=jnp.int32)
    begin = jnp.sum(jnp.where(member, starts[:, None, :], 0), axis=2)
    end = jnp.sum(jnp.where(member, ends[:, None, :], 0), axis=2)
    return segment, slot[None] - begin, end - 1 - slot[None]


def body(
    sizes, frames, item_lengths, frame_mask, first_norm, first_up, first_down, attend_norm,
    attend_joint, attend_out, conv_norm, conv_in, conv_kern, batch_gain, batch_bias, conv_out,
    second_norm, second_up, second_down, final_norm, output_grad,
):
    slots = frames.shape[1]
    x_at = lax.axis_index("fsdp").astype(jnp.int32).reshape(1)
    core = (lax.axis_index("dp") & 1).astype(jnp.int32).reshape(1)
    first_x = lax.axis_index("fsdp") == 0

    where = jnp.concatenate([x_at, core])
    line = Line()

    names = ("up1", "down1", "joint", "aout", "cin", "cout", "up2", "down2")
    shards = dict(
        zip(
            names,
            (first_up, first_down, attend_joint, attend_out, conv_in, conv_out, second_up, second_down),
        )
    )
    pieces = {}

    def cut_piece(name):
        piece = shards[name].shape[0] // 2
        pieces[name] = lax.dynamic_slice_in_dim(shards[name], core[0] * piece, piece, axis=0)

    cut_piece("up1")
    cut_piece("down1")
    line.did(pieces["up1"], pieces["down1"])
    vectors = (first_norm, attend_norm, conv_norm, batch_gain, batch_bias, second_norm, final_norm)
    vectors, conv_kern = line.after((vectors, conv_kern))
    norms = jnp.concatenate(
        [jnp.stack(vectors), jnp.zeros((1, D // 2), BF16), conv_kern.reshape(KER, D // 2)], axis=0
    )
    for name in names[2:]:
        cut_piece(name)
    partner = {"aout": "joint", "cout": "cin"}
    for name, host in partner.items():
        pieces[host] = jnp.concatenate([pieces[host], pieces.pop(name)], axis=1)
    names = tuple(name for name in names if name not in partner)
    near = {name: swap(pieces[name], "fsdp", 1, 2) for name in names[:2]}
    norms_o = swap(norms, "fsdp", 1, 2)
    near |= {name: swap(pieces[name], "fsdp", 1, 2) for name in names[2:]}
    far = {}

    def pass_on(*group):
        for name in group:
            far[name] = swap(line.after(near[name]), "dp", 1, sizes["dp"])

    def whole(name):
        host = partner.get(name, name)
        return shards[name], near[host], far[host]

    segment, position, left = layout(item_lengths[:, 0], frame_mask, slots)
    half = HDIM // 2
    freq = jnp.exp(jnp.arange(half, dtype=F32) * (-2.0 * math.log(10000.0) / HDIM))
    angle = position.astype(F32)[:, :, None] * freq
    cosine, sine = jnp.cos(angle), jnp.sin(angle)
    cos_t = jnp.concatenate([cosine] * 4, axis=-1)
    sin_t = jnp.concatenate([-sine, sine, -sine, sine], axis=-1)
    valid = frame_mask.astype(F32)

    def wide(values):
        return jnp.broadcast_to(values.astype(F32)[:, :, None], (MB, slots, 128))

    segb, before, after, validb = wide(segment), wide(position), wide(left), wide(valid)
    rows = jnp.stack([segment.astype(F32), valid], axis=1)
    near_end = jnp.minimum(position, left).reshape(MB, slots // CHUNK, CHUNK)
    inside = (jnp.min(near_end, axis=2) >= PAD).astype(jnp.int32)

    tables = (cos_t, sin_t, segb, before, after, validb, rows, inside)
    tables = lax.optimization_barrier((tables, tuple(pieces.values())))[0]
    cos_t, sin_t, segb, before, after, validb, rows, inside = tables
    line.did(rows, inside)
    norms_o = line.after(norms_o)
    first, second = jnp.where(first_x, norms, norms_o), jnp.where(first_x, norms_o, norms)
    gains = jnp.concatenate([first[:7], second[:7]], axis=1).astype(F32)
    kern = jnp.concatenate(
        [first[8:].reshape(KER // 2, D), second[8:].reshape(KER // 2, D)], axis=0
    ).astype(F32)
    g_first, g_attend, g_conv, g_bn, b_bn, g_second, g_final = (gains[i : i + 1] for i in range(7))
    line.did(gains)
    pass_on("up1", "down1")

    tall = MB * slots
    tm = 256
    x_flat = frames.reshape(tall, D)

    def row_spec(width):
        return pl.BlockSpec((tm, width), lambda i: (i, 0))

    x1, a1, h1, g1 = pl.pallas_call(
        feed_kernel,
        name="feed",
        grid=(tall // tm,),
        in_specs=[SMEM, row_spec(D), full((1, D)), *[ANY] * 6],
        out_specs=[row_spec(D), row_spec(D), row_spec(FF), row_spec(FF)],
        out_shape=[out((tall, D), F32), out((tall, D), BF16)] + [out((tall, FF), BF16)] * 2,
        scratch_shapes=weight_scratch((D, FF), (FF, D)),
        cost_estimate=cost(4 * tall * D * FF, 2e7),
    )(line.after(where), x_flat, g_first, *whole("up1"), *whole("down1"))
    line.did(a1)
    pass_on("joint")

    def cut(array):
        return array.reshape(MB, slots, array.shape[-1])

    def by_micro(*shape):
        rest = (0,) * len(shape)
        return pl.BlockSpec((1,) + shape, lambda i: (i,) + rest)

    x1 = cut(x1)
    x2, a2, qh, kh, vh, probs, mixed = pl.pallas_call(
        attend_kernel,
        name="attend",
        grid=(MB,),
        in_specs=[
            SMEM, by_micro(slots, D), full((1, D)), by_micro(slots, 128), by_micro(slots, 128),
            by_micro(slots, 128), by_micro(2, slots), *[ANY] * 6,
        ],
        out_specs=[by_micro(slots, D)] * 5 + [by_micro(HEADS, slots, slots), by_micro(slots, D)],
        out_shape=[out((MB, slots, D), F32)] + [out((MB, slots, D), BF16)] * 4
        + [out((MB, HEADS, slots, slots), BF16), out((MB, slots, D), BF16)],
        scratch_shapes=[
            pltpu.VMEM((D, 3 * D), BF16), pltpu.VMEM((D, D), BF16), pltpu.VMEM((slots, slots), F32),
            pltpu.SemaphoreType.DMA((6,)),
        ],
        cost_estimate=cost(MB * slots * (8 * D * D + 8 * slots * D), 3e7),
    )(line.after(where), x1, g_attend, cos_t, sin_t, segb, rows, *whole("joint"), *whole("aout"))
    line.did(a2)
    pass_on("cin")

    pad_rows = slots + 40

    tables_spec = [by_micro(slots, 128)] * 3
    a3, glu, p1, p2, conv, stats = pl.pallas_call(
        conv_kernel,
        name="conv",
        grid=(MB,),
        in_specs=[
            SMEM, SMEM, by_micro(slots, D), full((1, D)), full((KER, D)), *tables_spec, *[ANY] * 3,
        ],
        out_specs=[by_micro(slots, D)] * 5 + [by_micro(4, D)],
        out_shape=[
            out((MB, slots, D), BF16), out((MB, slots, D), F32), out((MB, slots, D), BF16),
            out((MB, slots, D), BF16), out((MB, slots, D), F32), out((MB, 4, D), F32),
        ],
        scratch_shapes=[
            pltpu.VMEM((D, 2 * D), BF16), pltpu.VMEM((pad_rows, D), F32),
            pltpu.VMEM((8, pad_rows - 8, D), F32), pltpu.SemaphoreType.DMA((3,)),
        ],
        cost_estimate=cost(MB * (4 * slots * D * D + 60 * KER * slots * D), 2e7),
    )(line.after(where), inside, x2, g_conv, kern, validb, before, after, *whole("cin"))
    stats = stats.reshape(4 * MB, D)
    line.did(stats)
    sync = Sum(line, sizes, stats)
    for _ in range(3):
        sync.step()
    pass_on("up2", "down2")
    while sync.step():
        pass
    total = sync.value.reshape(MB, 4, D)
    mid_gains = jnp.concatenate([g_bn, b_bn, g_second, g_final], axis=0)
    tiles = slots // tm

    def tile_spec(width):
        return pl.BlockSpec((tm, width), lambda m, i: (m * tiles + i, 0))

    def per_micro(rows_of):
        return pl.BlockSpec((1, rows_of, D), lambda m, *_: (m, 0, 0))

    enc, a4, e3, a5, h2, dz2, e4, db, dx3, mid_sums = pl.pallas_call(
        middle_kernel,
        name="middle",
        grid=(MB, tiles),
        in_specs=[SMEM, per_micro(4), full((4, D)), *[tile_spec(D)] * 3, *[ANY] * 9],
        out_specs=[tile_spec(D)] * 4 + [tile_spec(FF)] * 2 + [tile_spec(D)] * 3 + [per_micro(8)],
        out_shape=[out((tall, D), BF16)] * 4 + [out((tall, FF), BF16)] * 2
        + [out((tall, D), BF16)] + [out((tall, D), F32)] * 2 + [out((MB, 8, D), F32)],
        scratch_shapes=[
            pltpu.VMEM((D, D), BF16), pltpu.VMEM((D, FF), BF16), pltpu.VMEM((FF, D), BF16),
            pltpu.VMEM((tm, FF), BF16), pltpu.SemaphoreType.DMA((9,)),
        ],
        cost_estimate=cost(tall * (8 * D * FF + 4 * D * D), 4e7),
    )(line.after(where), total, mid_gains, conv.reshape(tall, D), x2.reshape(tall, D),
      output_grad.reshape(tall, D), *whole("cout"), *whole("up2"), *whole("down2"))
    stats = mid_sums[:, :2].reshape(2 * MB, D)
    line.did(stats)
    sync = Sum(line, sizes, stats)

    def product(*sides):
        found = []
        for side in sides:
            if isinstance(side, list):
                found.append([(array, 0) for array in side])
            else:
                found.append([(side.reshape(tall, side.shape[-1]), m) for m in range(MB)])
        return found

    def weights(name, *products):
        send = weight_call(name, products, line.after(1 - core), line, slots)
        got = swap(send, "dp", 1, sizes["dp"])
        return got, weight_call(name, products, line.after(core), line, slots)

    pair = weights("weights_second", product(h2, e4), product(a5, dz2), product(a4, e3))
    chain_a = Background(line, sizes, ((FF, D), (D, FF), (D, D)), *pair)
    while sync.step():
        pass
    chain_a.step()
    back = sync.value.reshape(MB, 2, D)
    back_gains = jnp.concatenate([g_bn, g_conv], axis=0)
    dg, dx2, e2, kern_sum, sums_conv = pl.pallas_call(
        conv_back_kernel,
        name="conv_back",
        grid=(MB,),
        in_specs=[
            SMEM, SMEM, per_micro(4), per_micro(2), full((2, D)), full((KER, D)),
            *[by_micro(slots, D)] * 7, *tables_spec, *[ANY] * 3,
        ],
        out_specs=[
            by_micro(slots, 2 * D), by_micro(slots, D), by_micro(slots, D), full((KER, D)), per_micro(8),
        ],
        out_shape=[
            out((MB, slots, 2 * D), BF16), out((MB, slots, D), F32), out((MB, slots, D), BF16),
            out((KER, D), F32), out((MB, 8, D), F32),
        ],
        scratch_shapes=[
            pltpu.VMEM((D, 2 * D), BF16), pltpu.VMEM((pad_rows, D), F32),
            pltpu.VMEM((8, pad_rows - 8, D), F32), pltpu.VMEM((slots, D), F32),
            pltpu.VMEM((KER, 8, D), F32), pltpu.SemaphoreType.DMA((3,)),
        ],
        cost_estimate=cost(MB * (4 * slots * D * D + 120 * KER * slots * D), 3e7),
    )(line.after(where), inside, total, back, back_gains, kern, conv, cut(db), glu, p1, p2, x2, cut(dx3),
      validb, before, after, *whole("cin"))
    line.did(sums_conv)
    pair = weights("weights_conv", product(a3, dg), product(mixed, e2))
    chain_c = Background(line, sizes, ((D, 2 * D), (D, D)), *pair)
    chain_a.step()
    chain_c.step()

    dj, dx1, e1, sums_attend = pl.pallas_call(
        attend_back_kernel,
        name="attend_back",
        grid=(MB,),
        in_specs=[
            SMEM, by_micro(slots, D), full((1, D)), *[by_micro(slots, 128)] * 2,
            *[by_micro(slots, D)] * 4, by_micro(HEADS, slots, slots), *[ANY] * 6,
        ],
        out_specs=[by_micro(slots, 3 * D), by_micro(slots, D), by_micro(slots, D), by_micro(8, D)],
        out_shape=[
            out((MB, slots, 3 * D), BF16), out((MB, slots, D), F32), out((MB, slots, D), BF16),
            out((MB, 8, D), F32),
        ],
        scratch_shapes=[
            pltpu.VMEM((D, 3 * D), BF16), pltpu.VMEM((D, D), BF16), pltpu.VMEM((slots, D), BF16),
            pltpu.VMEM((slots, D), F32), pltpu.VMEM((slots, D), F32), pltpu.SemaphoreType.DMA((6,)),
        ],
        cost_estimate=cost(MB * slots * (8 * D * D + 16 * slots * D), 3e7),
    )(line.after(where), x1, g_attend, cos_t, sin_t, dx2, qh, kh, vh, probs,
      *whole("joint"), *whole("aout"))
    line.did(sums_attend)
    chain_c.step()
    reduce_behind((chain_a, chain_c), sizes["dp"])
    pair = weights("weights_down", product(h1, e1), product(a2, dj))
    chain_d = Chain(line, sizes, ((FF, D), (D, 3 * D)), *pair, 3)
    dx1, e1 = dx1.reshape(tall, D), e1.reshape(tall, D)

    chain_d.step()
    fgrad, dz1, sums_first = pl.pallas_call(
        feed_back_kernel,
        name="feed_back",
        grid=(tall // tm,),
        in_specs=[
            SMEM, row_spec(D), full((1, D)), row_spec(D), row_spec(D), row_spec(FF), *[ANY] * 6,
        ],
        out_specs=[row_spec(D), row_spec(FF), full((8, D))],
        out_shape=[out((tall, D), BF16), out((tall, FF), BF16), out((8, D), F32)],
        scratch_shapes=weight_scratch((D, FF), (FF, D)),
        cost_estimate=cost(4 * tall * D * FF, 2e7),
    )(line.after(where), x_flat, g_first, dx1, e1, g1, *whole("up1"), *whole("down1"))
    line.did(sums_first)
    pair = weights("weights_up", product(a1, dz1))
    chain_f = Chain(line, sizes, ((D, FF),), *pair, 3)

    mid_sums = mid_sums[0] + mid_sums[1]
    small = jnp.concatenate(
        [
            kern_sum,
            sums_first[0:1],
            sums_attend[0, 0:1] + sums_attend[1, 0:1],
            sums_conv[0, 0:1] + sums_conv[1, 0:1],
            mid_sums[1:2],
            mid_sums[0:1],
            mid_sums[2:4],
            jnp.zeros((1, D), F32),
        ],
        axis=0,
    )
    line.did(small)
    small = Sum(line, sizes, small, (2,))
    chain_d.step()
    chain_f.step()
    small.step()
    small.step()
    chain_d.step()
    chain_d.step()
    chain_d.step()
    chain_f.step()
    small.step()
    chain_d.step()
    small.step()
    chain_f.step()
    chain_d.step()
    chain_f.step()
    chain_a.pass_on()
    chain_f.step()
    chain_d.step()
    small.step()
    chain_f.step()
    chain_a.step()
    chain_c.pass_on()
    chain_f.step()
    chain_d.step()
    chain_c.step()
    chain_f.step()
    chain_f.step()
    for chain in (chain_d, chain_f):
        while chain.plan:
            chain.step()
    while small.plan:
        small.step()
    small = small.value
    kern_grad = lax.dynamic_slice_in_dim(small, x_at[0] * (KER // 2), KER // 2, axis=0)
    vectors = lax.dynamic_slice_in_dim(small[KER:], x_at[0] * (D // 2), D // 2, axis=1)
    down2_g, up2_g, cout_g = chain_a.result
    cin_g, aout_g = chain_c.result
    down1_g, joint_g = chain_d.result
    (up1_g,) = chain_f.result
    return (
        enc.reshape(MB, slots, D), fgrad.reshape(MB, slots, D), vectors[0], up1_g, down1_g, vectors[1], joint_g, aout_g,
        vectors[2], cin_g, kern_grad, vectors[3], vectors[4], cout_g, vectors[5], up2_g, down2_g,
        vectors[6],
    )


def solution(mesh):
    split = P(None, ("dp", "fsdp"), None)
    row, mat = P("fsdp"), P("fsdp", None)
    weights = (row, mat, mat, row, mat, mat, row, mat, mat, row, row, mat, row, mat, mat, row)
    return jax.shard_map(
        functools.partial(body, dict(mesh.shape)),
        mesh=mesh,
        in_specs=(split, split, P(None, ("dp", "fsdp"))) + weights + (split,),
        out_specs=(split, split) + weights,
        check_vma=False,
    )
```
